32 devices in a mesh: dp: 2 (over core), expert: 4 (over y, x), seg: 4 (over z).
Axes of the slice: x: 2, y: 2, z: 4, core: 2. Of those that a mesh axis runs over, the one named last changes fastest.
Arguments:
- tokens: bfloat16 [512, 3072], P(('dp', 'expert'), 'seg'), parts along dimension 0, may hold values from -6 to 6
- expert_ids: int32 [512, 4], P(('dp', 'expert')), parts along dimension 0, may hold values from 0 to 15, as said below
- route_weight: float32 [512, 4], P(('dp', 'expert')), parts along dimension 0, may hold values from 0.1 to 1
- w_up: bfloat16 [16, 3072, 6144], P('expert', None, 'seg'), may hold values from -0.109375 to 0.109375
- w_down: bfloat16 [16, 6144, 3072], P('expert', 'seg'), may hold values from -0.078125 to 0.078125
Outputs:
- mixed: bfloat16 [512, 3072], P(('dp', 'expert'), 'seg'), parts along dimension 0
The draws below stay inside these ranges and needn't reach their ends.
There are 2 independent parts, one for each index of `dp`. The reference program is written for one: setup_inputs(seed, part) draws one part's arguments, and reference() takes and returns one part's arrays. A program takes and returns all parts, laid end to end along the dimension named above; an argument that names none is the same for every part. Nothing has to cross between parts.
Inputs may be any that keep to these rules, and one draw needn't show every extreme that they name: `expert_ids`: each row names 4 different experts. Within each aligned block of 64 rows (the rows of one device), no expert is named by more than 21 rows, and one expert is named by exactly 21 rows in every block.
All inputs are finite; a program needn't handle non-finite values.
Results may differ from the reference program's by a relative error of at most 0.0049.
Values may be sent and summed in bfloat16 or wider, within the bound.
No kernel may reach another device: no remote copies, remote signals or barrier semaphores. Data moves between devices by JAX's collectives and lax.ppermute only.
A program may use at most 128 MiB of HBM per device.

```python
import math
import jax
import jax.numpy as jnp
from jax import lax

D = 3072
FF = 6144
EXPERTS = 16
TOPK = 4
TOK_DEV = 64
SEND_CAP = 21
TOKENS = 256


def draw_expert_ids(key, part):
    blocks = TOKENS // TOK_DEV
    key_hot, key_rows = jax.random.split(jax.random.fold_in(key, 11), 2)
    hottest = jax.random.randint(key_hot, (), 0, EXPERTS)
    column = jnp.arange(TOPK, dtype=jnp.int32)[None, :]

    def one_block(block_key):
        key_first, key_second, key_third = jax.random.split(block_key, 3)
        chosen = jax.random.permutation(key_first, TOK_DEV)
        has_hot = jnp.zeros((TOK_DEV,), jnp.int32).at[chosen[:SEND_CAP]].set(1)
        others = TOPK - has_hot
        offset = jnp.cumsum(others) - others
        order = jax.random.permutation(key_second, EXPERTS - 1)
        picks = order[(offset[:, None] + column) % (EXPERTS - 1)]
        picks = picks + (picks >= hottest).astype(jnp.int32)
        shifted = jnp.concatenate([jnp.full((TOK_DEV, 1), hottest, jnp.int32), picks[:, :TOPK - 1]], axis=1)
        chosen_rows = jnp.where(has_hot[:, None] == 1, shifted, picks)
        turned = jax.random.randint(key_third, (TOK_DEV, 1), 0, TOPK)
        return jnp.take_along_axis(chosen_rows, (column + turned) % TOPK, axis=1)
    keys = jax.random.split(key_rows, blocks)
    return jax.vmap(one_block)(keys).reshape(TOKENS, TOPK).astype(jnp.int32)


def steps_of(stream_key, extent, cuts, low, largest):
    def one(axis_at, parts):
        draws = jax.random.uniform(jax.random.fold_in(jax.random.fold_in(stream_key, 6), axis_at), (parts,), jnp.float32, low / len(cuts), largest / len(cuts))
        return jnp.repeat(jnp.exp(draws), extent[axis_at] // parts).reshape((-1,) + (1,) * (len(extent) - axis_at - 1))

    loudness = one(*cuts[0])
    for cut in cuts[1:]:
        loudness = loudness * one(*cut)
    return loudness


def bell_draw(key, dims, width, reach, shards=(), kind=jnp.bfloat16):
    gain = steps_of(key, dims, shards, -0.22, 0.18) if shards else 1.0
    drawn = jax.random.normal(key, dims, jnp.float32) * width * gain
    return jnp.minimum(jnp.maximum(drawn, -reach), reach).astype(kind)


def setup_inputs(seed: int = 0, part: int = 0) -> dict:
    splits = jax.random.split(jax.random.key(seed), 6)
    part_splits = jax.random.split(jax.random.fold_in(splits[5], part), 6)
    return {
        "tokens": bell_draw(part_splits[0], (TOKENS, D), 1.0, 6.0, ((0, 4), (1, 4))),
        "expert_ids": draw_expert_ids(jax.random.fold_in(jax.random.fold_in(splits[5], part), 71), part),
        "route_weight": jnp.clip(jnp.exp(math.log(1.0) - 2.3025851 * jax.random.uniform(part_splits[2], (TOKENS, TOPK), jnp.float32) ** steps_of(part_splits[2], (TOKENS, TOPK), ((0, 4),), -0.2, 0.2)), 0.1, 1.0),
        "w_up": bell_draw(splits[3], (EXPERTS, D, FF), D ** -0.5, 0.109375, ((0, 4), (2, 4))),
        "w_down": bell_draw(splits[4], (EXPERTS, FF, D), FF ** -0.5, 0.078125, ((0, 4), (1, 4))),
    }


def reference(tokens, expert_ids, route_weight, w_up, w_down):
    tok_all = tokens.shape[0]
    topk = expert_ids.shape[1]
    blocks = tok_all // TOK_DEV
    grouped = expert_ids.reshape(blocks, TOK_DEV * topk)
    onehot = (grouped[:, :, None] == jnp.arange(EXPERTS, dtype=jnp.int32)[None, None, :]).astype(jnp.int32)
    before = jnp.cumsum(onehot, axis=1) - onehot
    slot = jnp.sum(before * onehot, axis=2)
    source = jnp.arange(blocks, dtype=jnp.int32)[:, None]
    dest = (source * SEND_CAP + slot).reshape(-1).astype(jnp.int32)
    flat_route = expert_ids.reshape(-1)
    repeated = jnp.repeat(tokens, topk, axis=0)
    norm_weight = route_weight / jnp.sum(route_weight, axis=1, keepdims=True)
    flat_weight = norm_weight.reshape(-1)
    cap_rows = blocks * SEND_CAP

    def one_expert(total, inputs):
        expert, up_weight, down_weight = inputs
        mine = flat_route == expert
        index = jnp.where(mine, dest, cap_rows).astype(jnp.int32)
        buffer = jnp.zeros((cap_rows, tokens.shape[1]), jnp.bfloat16).at[index].set(repeated, mode="drop")
        up_sum = jnp.dot(buffer, up_weight, preferred_element_type=jnp.float32)
        hidden = jax.nn.silu(up_sum).astype(jnp.bfloat16)
        result = jnp.dot(hidden, down_weight, preferred_element_type=jnp.float32)
        picked = result[jnp.minimum(index, cap_rows - 1)]
        factor = jnp.where(mine, flat_weight, jnp.zeros_like(flat_weight))
        return total + picked * factor[:, None], None

    start = jnp.zeros((tok_all * topk, tokens.shape[1]), jnp.float32)
    total, _ = lax.scan(one_expert, start, (jnp.arange(EXPERTS, dtype=jnp.int32), w_up, w_down))
    return total.reshape(tok_all, topk, tokens.shape[1]).sum(axis=1).astype(jnp.bfloat16)
```

```python
import functools

import jax
import jax.numpy as jnp
from jax import lax
from jax.experimental import pallas as pl
from jax.experimental.pallas import tpu as pltpu
from jax.sharding import PartitionSpec as P

SEND_CAP = 21
LANES = 128


def hop(value, axis, k):
    n = lax.axis_size(axis)
    return lax.ppermute(value, axis, [(i, i ^ k) for i in range(n)])


def up_to(value, multiple):
    return -(-value // multiple) * multiple


def expert_kernel(
    sizes, place, *refs
):
    (n_exp, n_seg, n_loc, rows, tok, col_a, col_b, tile_f, tile_d, topk) = sizes
    xa = refs[:n_exp]
    xb = refs[n_exp:n_exp + n_seg]
    meta, w_up, w_down = refs[n_exp + n_seg:n_exp + n_seg + 3]
    outs = refs[n_exp + n_seg + 3:]
    ca = outs[:n_exp]
    cb = outs[n_exp:n_exp + n_seg]
    packed, hidden, pick, pick_t, row_w = outs[n_exp + n_seg:]
    step = pl.program_id(0)
    seg_at = place[0]
    first_expert = place[1] * n_loc
    tokens = n_exp * tok
    ff = w_up.shape[2] * (hidden.shape[1] // w_up.shape[2])
    per_expert = ff // tile_f
    n_up = n_loc * per_expert
    slice_d = col_a + col_b
    tiles_a = col_a // tile_d
    tiles_b = col_b // tile_d
    n_a = n_seg * tiles_a

    @pl.when(step == 0)
    def _():
        info = meta[...].astype(jnp.float32)
        ids = info[:topk]
        weights = info[topk:2 * topk] + info[2 * topk:3 * topk]
        masks = []
        gains = []
        for e in range(n_loc):
            here = (ids == (first_expert + e).astype(jnp.float32)).astype(jnp.float32)
            masks.append(jnp.sum(here, axis=0, keepdims=True))
            gains.append(jnp.sum(here * weights, axis=0, keepdims=True))
        earlier = (
            lax.broadcasted_iota(jnp.int32, (tokens, tokens), 0)
            < lax.broadcasted_iota(jnp.int32, (tokens, tokens), 1)
        ).astype(jnp.float32).astype(jnp.bfloat16)
        slot_of_row = lax.broadcasted_iota(jnp.int32, (rows, tokens), 0).astype(jnp.float32)
        for e in range(n_loc):
            mask = jnp.broadcast_to(masks[e], (16, tokens))
            before = jnp.dot(mask.astype(jnp.bfloat16), earlier, preferred_element_type=jnp.float32)
            chosen = jnp.where(
                (slot_of_row == before[:1]) & (masks[e] > 0.5), 1.0, 0.0
            )
            pick[e * rows:(e + 1) * rows, :] = chosen.astype(jnp.bfloat16)
            row_w[e * rows:(e + 1) * rows, :] = jnp.sum(chosen * gains[e], axis=1, keepdims=True)
        pick_t[...] = jnp.transpose(pick[...].astype(jnp.float32)).astype(jnp.bfloat16)
        for j in range(n_seg):
            at = pl.multiple_of((seg_at ^ j) * slice_d, LANES)
            part = None
            for k in range(n_exp):
                piece = jnp.dot(
                    pick[:, k * tok:(k + 1) * tok], xa[k][:, j * col_a:(j + 1) * col_a],
                    preferred_element_type=jnp.float32,
                )
                part = piece if part is None else part + piece
            packed[:, pl.ds(at, col_a)] = part.astype(jnp.bfloat16)
            part = jnp.dot(pick[...], xb[j][...], preferred_element_type=jnp.float32)
            packed[:, pl.ds(pl.multiple_of(at + col_a, LANES), col_b)] = part.astype(jnp.bfloat16)

    for e in range(n_loc):
        for f in range(per_expert):
            @pl.when(step == e * per_expert + f)
            def _(e=e, f=f):
                up = jnp.dot(
                    packed[e * rows:(e + 1) * rows, :], w_up[0], preferred_element_type=jnp.float32
                )
                act = up / (1.0 + jnp.exp(-up))
                hidden[e * rows:(e + 1) * rows, f * tile_f:(f + 1) * tile_f] = act.astype(jnp.bfloat16)

    def down():
        total = None
        for e in range(n_loc):
            at = slice(e * rows, (e + 1) * rows)
            result = jnp.dot(hidden[at, :], w_down[e], preferred_element_type=jnp.float32)
            result = result * row_w[at, :]
            high = result.astype(jnp.bfloat16)
            low = (result - high.astype(jnp.float32)).astype(jnp.bfloat16)
            back = pick_t[:, at]
            part = jnp.dot(back, high, preferred_element_type=jnp.float32)
            part = part + jnp.dot(back, low, preferred_element_type=jnp.float32)
            total = part if total is None else total + part
        return total

    @pl.when((step >= n_up) & (step < n_up + n_a))
    def _():
        total = down()
        for k in range(n_exp):
            ca[k][...] = total[k * tok:(k + 1) * tok].astype(jnp.bfloat16)

    for j in range(n_seg):
        for b in range(tiles_b):
            @pl.when(step == n_up + n_a + j * tiles_b + b)
            def _(j=j, b=b):
                cb[j][:, b * tile_d:(b + 1) * tile_d] = down().astype(jnp.bfloat16)


def experts(place, xa, xb, meta, w_up, w_down, topk):
    n_exp, n_seg = len(xa), len(xb)
    n_loc, width, ff = w_up.shape
    tok = xa[0].shape[0]
    col_a = xa[0].shape[1] // n_seg
    col_b = xb[0].shape[1]
    tokens = n_exp * tok
    rows = up_to(SEND_CAP * n_exp, 16)
    tile_f = ff // 2
    tile_d = col_b
    slice_d = col_a + col_b
    per_expert = ff // tile_f
    n_up = n_loc * per_expert
    tiles_a = col_a // tile_d
    tiles_b = col_b // tile_d
    n_a = n_seg * tiles_a
    n_b = n_seg * tiles_b
    per_slice = slice_d // tile_d

    def up_at(i, place):
        i = jnp.minimum(i, n_up - 1)
        return i // per_expert, 0, i % per_expert

    def down_at(i, place):
        i = jnp.maximum(i - n_up, 0)
        j_a = jnp.minimum(i // tiles_a, n_seg - 1)
        at_a = (place[0] ^ j_a) * per_slice + i % tiles_a
        late = jnp.maximum(i - n_a, 0)
        j_b = late // tiles_b
        at_b = (place[0] ^ j_b) * per_slice + tiles_a + late % tiles_b
        return 0, 0, jnp.where(i < n_a, at_a, at_b)

    def a_at(i, place):
        return 0, jnp.clip(i - n_up, 0, n_a - 1)

    whole = lambda i, place: (0, 0)
    sizes = (n_exp, n_seg, n_loc, rows, tok, col_a, col_b, tile_f, tile_d, topk)
    grid_spec = pltpu.PrefetchScalarGridSpec(
        num_scalar_prefetch=1,
        grid=(n_up + n_a + n_b,),
        in_specs=[pl.BlockSpec(x.shape, whole) for x in xa]
        + [pl.BlockSpec(x.shape, whole) for x in xb]
        + [
            pl.BlockSpec(meta.shape, whole),
            pl.BlockSpec((1, width, tile_f), up_at),
            pl.BlockSpec((n_loc, ff, tile_d), down_at),
        ],
        out_specs=[pl.BlockSpec((tok, tile_d), a_at) for _ in xa]
        + [pl.BlockSpec((tokens, col_b), whole) for _ in xb],
        scratch_shapes=[
            pltpu.VMEM((n_loc * rows, width), jnp.bfloat16),
            pltpu.VMEM((n_loc * rows, ff), jnp.bfloat16),
            pltpu.VMEM((n_loc * rows, tokens), jnp.bfloat16),
            pltpu.VMEM((tokens, n_loc * rows), jnp.bfloat16),
            pltpu.VMEM((n_loc * rows, 1), jnp.float32),
        ],
    )
    outs = pl.pallas_call(
        functools.partial(expert_kernel, sizes),
        grid_spec=grid_spec,
        out_shape=[jax.ShapeDtypeStruct(x.shape, jnp.bfloat16) for x in xa]
        + [jax.ShapeDtypeStruct(x.shape, jnp.bfloat16) for x in xb],
        compiler_params=pltpu.CompilerParams(vmem_limit_bytes=48 << 20),
    )(place, *xa, *xb, meta, w_up, w_down)
    return outs[:n_exp], outs[n_exp:]


def total_of(parts):
    total = parts[0].astype(jnp.float32)
    for part in parts[1:]:
        total = total + part.astype(jnp.float32)
    return total


def shards(tokens, expert_ids, route_weight, w_up, w_down):
    n_exp = lax.axis_size("expert")
    n_seg = lax.axis_size("seg")
    tok, slice_d = tokens.shape
    topk = expert_ids.shape[1]
    if slice_d % (3 * LANES):
        return plain(tokens, expert_ids, route_weight, w_up, w_down)
    col_b = slice_d // 3
    col_a = slice_d - col_b
    place = jnp.stack([lax.axis_index("seg"), lax.axis_index("expert")]).astype(jnp.int32)

    norm = route_weight / jnp.sum(route_weight, axis=1, keepdims=True)
    high = lax.reduce_precision(norm, 8, 7)
    low = norm - high
    info = jnp.concatenate([expert_ids.astype(jnp.float32), high, low], axis=1).T
    info = jnp.pad(info.astype(jnp.bfloat16), ((0, up_to(3 * topk, 16) - 3 * topk), (0, col_b - tok)))

    first_a = tokens[:, :col_a]
    first_b = jnp.concatenate([tokens[:, col_a:], info], axis=0)
    got_a = {k: hop(first_a, "seg", k) for k in reversed(range(1, n_seg))}
    got_b = {k: hop(first_b, "expert", k) for k in reversed(range(1, n_exp))}
    mine_a = jnp.concatenate([first_a] + [got_a[k] for k in range(1, n_seg)], axis=1)
    all_b = [first_b] + [got_b[k] for k in range(1, n_exp)]
    mine_b = jnp.concatenate([b[:tok] for b in all_b], axis=0)
    meta = jnp.concatenate([b[tok:, :tok] for b in all_b], axis=1)
    xa = {k: hop(mine_a, "expert", k) for k in reversed(range(1, n_exp))}
    xb = {k: hop(mine_b, "seg", k) for k in reversed(range(1, n_seg))}
    xa[0], xb[0] = mine_a, mine_b

    ca, cb = experts(
        place, [xa[k] for k in range(n_exp)], [xb[k] for k in range(n_seg)], meta, w_up, w_down, topk
    )

    ra = {k: hop(ca[k], "expert", k) for k in reversed(range(1, n_exp))}
    rb = {k: hop(cb[k], "seg", k) for k in reversed(range(1, n_seg))}
    sum_a = total_of([ca[0]] + [ra[k] for k in range(1, n_exp)])
    sum_b = total_of([cb[0]] + [rb[k] for k in range(1, n_seg)])
    part_a = [sum_a[:, j * col_a:(j + 1) * col_a] for j in range(n_seg)]
    part_b = [sum_b[k * tok:(k + 1) * tok] for k in range(n_exp)]
    fa = {j: hop(part_a[j].astype(jnp.bfloat16), "seg", j) for j in reversed(range(1, n_seg))}
    fb = {k: hop(part_b[k].astype(jnp.bfloat16), "expert", k) for k in reversed(range(1, n_exp))}
    out_a = total_of([part_a[0]] + [fa[j] for j in range(1, n_seg)])
    out_b = total_of([part_b[0]] + [fb[k] for k in range(1, n_exp)])
    return jnp.concatenate([out_a, out_b], axis=1).astype(jnp.bfloat16)


def plain(tokens, expert_ids, route_weight, w_up, w_down):
    n_exp = lax.axis_size("expert")
    exp_local, width = w_up.shape[:2]
    n_experts = n_exp * exp_local
    topk = expert_ids.shape[1]
    tok_rows, width_seg = tokens.shape
    flat = expert_ids.reshape(-1)
    onehot = (flat[:, None] == jnp.arange(n_experts, dtype=jnp.int32)[None, :]).astype(jnp.int32)
    before = jnp.cumsum(onehot, axis=0) - onehot
    target = flat * SEND_CAP + jnp.sum(before * onehot, axis=1)
    norm_weight = route_weight / jnp.sum(route_weight, axis=1, keepdims=True)
    buffer = jnp.zeros((n_experts * SEND_CAP, width_seg), tokens.dtype)
    packed = buffer.at[target].set(jnp.repeat(tokens, topk, axis=0))
    packed = packed.reshape(n_exp, exp_local * SEND_CAP, width_seg)
    arrived = lax.all_to_all(packed, "expert", split_axis=0, concat_axis=0, tiled=True)
    piece = lax.all_gather(arrived, "seg", axis=2, tiled=True)
    block = piece.reshape(n_exp, exp_local, SEND_CAP, width)
    up_sum = jnp.einsum("sekd,edf->eskf", block, w_up, preferred_element_type=jnp.float32)
    hidden = jax.nn.silu(up_sum).astype(jnp.bfloat16)
    partial_out = jnp.einsum("eskf,efd->sekd", hidden, w_down, preferred_element_type=jnp.float32)
    partial_out = partial_out.reshape(n_exp, exp_local * SEND_CAP, width)
    returned = lax.all_to_all(partial_out, "expert", split_axis=0, concat_axis=0, tiled=True)
    picked = returned.reshape(n_experts * SEND_CAP, width)[target]
    weighted = (picked * norm_weight.reshape(-1)[:, None]).reshape(tok_rows, topk, width).sum(axis=1)
    return lax.psum_scatter(weighted, "seg", scatter_dimension=1, tiled=True).astype(jnp.bfloat16)


def solution(mesh):
    placed = (
        P(("dp", "expert"), "seg"),
        P(("dp", "expert"), None),
        P(("dp", "expert"), None),
        P("expert", None, "seg"),
        P("expert", "seg", None),
    )
    return jax.shard_map(
        shards, mesh=mesh, in_specs=placed, out_specs=P(("dp", "expert"), "seg"), check_vma=False
    )
```

```python
import functools

import jax
import jax.numpy as jnp
from jax import lax
from jax.experimental import pallas as pl
from jax.experimental.pallas import tpu as pltpu
from jax.sharding import PartitionSpec as P


SEND_CAP = 21
LANES = 128


def hop(value, axis, k):
    n = lax.axis_size(axis)
    return lax.ppermute(value, axis, [(i, i ^ k) for i in range(n)])


def up_to(value, multiple):
    return -(-value // multiple) * multiple


def call(body, ins, outs, scratch, limit, flops=0, moved=0):
    return pl.pallas_call(
        body,
        in_specs=[pl.BlockSpec(memory_space=space) for _, space in ins],
        out_specs=[pl.BlockSpec(memory_space=pltpu.VMEM) for _ in outs],
        out_shape=outs,
        scratch_shapes=scratch,
        compiler_params=pltpu.CompilerParams(vmem_limit_bytes=limit << 20),
        cost_estimate=pl.CostEstimate(flops=flops, bytes_accessed=moved, transcendentals=0),
    )(*[value for value, _ in ins])


def first_kernel(topk, col_a, place, tokens, ids, route, out_a, out_b):
    tok = tokens.shape[0]
    col_b = out_b.shape[1]
    out_a[...] = tokens[:, :col_a]
    out_b[:tok, :] = tokens[:, col_a:]
    weight = route[...]
    norm = weight / jnp.sum(weight, axis=0, keepdims=True)
    high = norm.astype(jnp.bfloat16).astype(jnp.float32)
    info = jnp.concatenate([ids[...].astype(jnp.float32), high, norm - high], axis=0)
    rows = out_b.shape[0] - tok
    info = jnp.concatenate([info, jnp.zeros((rows - 3 * topk, tok), jnp.float32)], axis=0)
    info = jnp.concatenate([info, jnp.zeros((rows, col_b - tok), jnp.float32)], axis=1)
    out_b[tok:, :] = info.astype(jnp.bfloat16)


def fetch_kernel(lo, w_ref, after, *refs):
    outs, sem = refs[:-1], refs[-1]
    copies = [
        pltpu.make_async_copy(w_ref.at[lo + i], out, sem.at[i]) for i, out in enumerate(outs)
    ]
    for copy in copies:
        copy.start()
    for copy in copies:
        copy.wait()


def fetch(w, lo, hi, after):
    return call(
        functools.partial(fetch_kernel, lo),
        [(w, pltpu.HBM), (after, pltpu.HBM)], [pltpu.VMEM(w.shape[1:], w.dtype)] * (hi - lo),
        [pltpu.SemaphoreType.DMA((hi - lo,))], 20, moved=2 * w[0].size * (hi - lo),
    )


def route_rows(meta, n_loc, rows, topk, first_expert, pick, pick_t, row_w):
    tokens = pick.shape[1]
    info = meta[...].astype(jnp.float32)
    ids = info[:topk]
    weights = info[topk:2 * topk] + info[2 * topk:3 * topk]
    earlier = (
        lax.broadcasted_iota(jnp.int32, (tokens, tokens), 0)
        < lax.broadcasted_iota(jnp.int32, (tokens, tokens), 1)
    ).astype(jnp.float32).astype(jnp.bfloat16)
    slot_of_row = lax.broadcasted_iota(jnp.int32, (rows, tokens), 0).astype(jnp.float32)
    for e in range(n_loc):
        here = (ids == (first_expert + e).astype(jnp.float32)).astype(jnp.float32)
        mask = jnp.sum(here, axis=0, keepdims=True)
        gain = jnp.sum(here * weights, axis=0, keepdims=True)
        before = jnp.dot(
            jnp.broadcast_to(mask, (16, tokens)).astype(jnp.bfloat16), earlier,
            preferred_element_type=jnp.float32,
        )
        chosen = jnp.where((slot_of_row == before[:1]) & (mask > 0.5), 1.0, 0.0)
        pick[e * rows:(e + 1) * rows, :] = chosen.astype(jnp.bfloat16)
        row_w[e * rows:(e + 1) * rows, :] = jnp.sum(chosen * gain, axis=1, keepdims=True)
    pick_t[...] = jnp.transpose(pick[...].astype(jnp.float32)).astype(jnp.bfloat16)


def down_tile(hidden, weight, pick_t, row_w, rows):
    total = None
    for e in range(weight.shape[0]):
        at = slice(e * rows, (e + 1) * rows)
        result = jnp.dot(hidden[at, :], weight[e], preferred_element_type=jnp.float32)
        result = result * row_w[at, :]
        high = result.astype(jnp.bfloat16)
        low = (result - high.astype(jnp.float32)).astype(jnp.bfloat16)
        back = pick_t[:, at]
        part = jnp.dot(back, high, preferred_element_type=jnp.float32)
        part = part + jnp.dot(back, low, preferred_element_type=jnp.float32)
        total = part if total is None else total + part
    return total


def columns_of(w_down, at, wide):
    return w_down.at[:, :, pl.ds(pl.multiple_of(at, LANES), wide)]


def up_kernel(sizes, place, *refs):
    n_exp, n_seg, n_loc, rows, tok, col_a, col_b, tile_f, topk, n_held = sizes
    xa, refs = refs[:n_exp], refs[n_exp:]
    xb, refs = refs[:n_seg], refs[n_seg:]
    meta, refs = refs[0], refs[1:]
    w_held, refs = refs[:n_held], refs[n_held:]
    (w_up, w_down), refs = refs[:2], refs[2:]
    cb, refs = refs[:n_seg], refs[n_seg:]
    hidden, pick_t, row_w, pick, joined, packed, buf_u, buf_d, sem_u, sem_d = refs
    seg_at = place[0]
    slice_d = col_a + col_b
    per = w_up.shape[2] // tile_f
    tiles = (n_loc - n_held) * per
    deep_u, deep_d = buf_u.shape[0], buf_d.shape[0]

    def tile_u(t):
        cols = pl.ds(pl.multiple_of(lax.rem(t, per) * tile_f, LANES), tile_f)
        slot = lax.rem(t, deep_u)
        return pltpu.make_async_copy(
            w_up.at[n_held + lax.div(t, per), :, cols], buf_u.at[slot], sem_u.at[slot]
        )

    def tile_d(j):
        slot = lax.rem(j, deep_d)
        return pltpu.make_async_copy(
            columns_of(w_down, (seg_at ^ j) * slice_d + col_a, col_b), buf_d.at[slot], sem_d.at[slot]
        )

    for t in range(min(deep_u, tiles)):
        tile_u(jnp.int32(t)).start()
    for j in range(min(deep_d, n_seg)):
        tile_d(jnp.int32(j)).start()
    for k in range(n_exp):
        joined[k * tok:(k + 1) * tok, :] = xa[k][...]
    route_rows(meta, n_loc, rows, topk, place[1] * n_loc, pick, pick_t, row_w)
    for j in range(n_seg):
        at = pl.multiple_of((seg_at ^ j) * slice_d, LANES)
        part = jnp.dot(
            pick[...], joined[:, j * col_a:(j + 1) * col_a], preferred_element_type=jnp.float32
        )
        packed[:, pl.ds(at, col_a)] = part.astype(jnp.bfloat16)
        part = jnp.dot(pick[...], xb[j][...], preferred_element_type=jnp.float32)
        packed[:, pl.ds(pl.multiple_of(at + col_a, LANES), col_b)] = part.astype(jnp.bfloat16)

    def up(at, f, weight):
        value = jnp.dot(packed[at, :], weight, preferred_element_type=jnp.float32)
        value = value / (1.0 + jnp.exp(-value))
        cols = pl.ds(pl.multiple_of(f * tile_f, LANES), tile_f)
        hidden[at, cols] = value.astype(jnp.bfloat16)

    for e, held in enumerate(w_held):
        def from_held(f, carry, e=e, held=held):
            cols = pl.ds(pl.multiple_of(f * tile_f, LANES), tile_f)
            up(slice(e * rows, (e + 1) * rows), f, held[:, cols])
            return carry

        lax.fori_loop(0, per, from_held, 0)

    def from_ring(t, carry):
        tile_u(t).wait()
        at = pl.ds(pl.multiple_of((n_held + lax.div(t, per)) * rows, 16), rows)
        up(at, lax.rem(t, per), buf_u[lax.rem(t, deep_u)])

        @pl.when(t + deep_u < tiles)
        def _():
            tile_u(t + deep_u).start()

        return carry

    lax.fori_loop(0, tiles, from_ring, 0)

    def down(j, carry):
        tile_d(j).wait()
        total = down_tile(hidden, buf_d.at[lax.rem(j, deep_d)], pick_t, row_w, rows).astype(jnp.bfloat16)
        for i in range(n_seg):
            @pl.when(j == i)
            def _(i=i):
                cb[i][...] = total

        @pl.when(j + deep_d < n_seg)
        def _():
            tile_d(j + deep_d).start()

        return carry

    lax.fori_loop(0, n_seg, down, 0)


def down_kernel(sizes, place, hidden, pick_t, row_w, w_down, *refs):
    n_exp, n_seg, rows, tok, slice_d, lo = sizes
    ca = refs[:n_exp]
    buf, sem = refs[n_exp:]
    deep, wide = buf.shape[0], buf.shape[3]

    def tile_d(j):
        slot = lax.rem(j, deep)
        return pltpu.make_async_copy(
            columns_of(w_down, (place[0] ^ j) * slice_d + lo, wide), buf.at[slot], sem.at[slot]
        )

    for j in range(min(deep, n_seg)):
        tile_d(jnp.int32(j)).start()

    def down(j, carry):
        tile_d(j).wait()
        total = down_tile(hidden, buf.at[lax.rem(j, deep)], pick_t, row_w, rows).astype(jnp.bfloat16)
        for k in range(n_exp):
            ca[k][:, pl.ds(pl.multiple_of(j * wide, LANES), wide)] = total[k * tok:(k + 1) * tok]

        @pl.when(j + deep < n_seg)
        def _():
            tile_d(j + deep).start()

        return carry

    lax.fori_loop(0, n_seg, down, 0)


def experts_up(place, xa, xb, meta, w_held, w_up, w_down, topk):
    n_exp, n_seg = len(xa), len(xb)
    n_loc, ff, width = w_down.shape
    tok = xa[0].shape[0]
    col_a = xa[0].shape[1] // n_seg
    col_b = xb[0].shape[1]
    tokens = n_exp * tok
    rows = up_to(SEND_CAP * n_exp, 16)
    sizes = (n_exp, n_seg, n_loc, rows, tok, col_a, col_b, ff // 3, topk, len(w_held))
    bf16 = jnp.bfloat16
    vmem = lambda values: [(value, pltpu.VMEM) for value in values]
    outs = call(
        functools.partial(up_kernel, sizes),
        [(place, pltpu.SMEM)] + vmem(xa) + vmem(xb) + vmem([meta]) + vmem(w_held)
        + [(w_up, pltpu.HBM), (w_down, pltpu.HBM)],
        [jax.ShapeDtypeStruct((tokens, col_b), bf16)] * n_seg
        + [jax.ShapeDtypeStruct((n_loc * rows, ff), bf16),
           jax.ShapeDtypeStruct((tokens, n_loc * rows), bf16),
           jax.ShapeDtypeStruct((n_loc * rows, 1), jnp.float32)],
        [pltpu.VMEM((n_loc * rows, tokens), bf16),
         pltpu.VMEM((tokens, n_seg * col_a), bf16),
         pltpu.VMEM((n_loc * rows, width), bf16),
         pltpu.VMEM((3, width, ff // 3), bf16),
         pltpu.VMEM((3, n_loc, ff, col_b), bf16),
         pltpu.SemaphoreType.DMA((3,)),
         pltpu.SemaphoreType.DMA((3,))],
        24, flops=2 * n_loc * 256 * width * ff, moved=2 * n_loc * ff * col_b * n_seg,
    )
    return outs[:n_seg], outs[n_seg:]


def experts_down(place, held, w_down, lo, wide, tok, n_exp, n_seg, slice_d):
    n_loc, ff, _ = w_down.shape
    hidden, pick_t, row_w = held
    rows = hidden.shape[0] // n_loc
    return call(
        functools.partial(down_kernel, (n_exp, n_seg, rows, tok, slice_d, lo)),
        [(place, pltpu.SMEM), (hidden, pltpu.VMEM), (pick_t, pltpu.VMEM), (row_w, pltpu.VMEM),
         (w_down, pltpu.HBM)],
        [jax.ShapeDtypeStruct((tok, n_seg * wide), jnp.bfloat16)] * n_exp,
        [pltpu.VMEM((n_seg, n_loc, ff, wide), jnp.bfloat16), pltpu.SemaphoreType.DMA((n_seg,))],
        20, flops=2 * n_loc * 256 * n_seg * wide * ff, moved=2 * n_loc * ff * wide * n_seg,
    )


def total_of(parts):
    total = parts[0].astype(jnp.float32)
    for part in parts[1:]:
        total = total + part.astype(jnp.float32)
    return total


def staged(tokens, expert_ids, route_weight, w_up, w_down):
    n_exp = lax.axis_size("expert")
    n_seg = lax.axis_size("seg")
    tok, slice_d = tokens.shape
    topk = expert_ids.shape[1]
    col_b = slice_d // 3
    col_a = slice_d - col_b
    place = jnp.stack([lax.axis_index("seg"), lax.axis_index("expert")]).astype(jnp.int32)

    tok_rows = up_to(3 * topk, 16)
    first_a, first_b = call(
        functools.partial(first_kernel, topk, col_a),
        [(place, pltpu.SMEM), (tokens, pltpu.VMEM), (expert_ids.T, pltpu.VMEM),
         (route_weight.T, pltpu.VMEM)],
        [jax.ShapeDtypeStruct((tok, col_a), jnp.bfloat16),
         jax.ShapeDtypeStruct((tok + tok_rows, col_b), jnp.bfloat16)],
        [], 2,
    )
    n_loc = w_up.shape[0]
    cut, held_loc = n_loc // 4, n_loc // 2
    got_a = {k: hop(first_a, "seg", k) for k in reversed(range(1, n_seg))}
    got_b = {k: hop(first_b, "expert", k) for k in reversed(range(1, n_exp))}
    up_1 = fetch(w_up, 0, cut, first_a)
    mine_a = jnp.concatenate([first_a] + [got_a[k] for k in range(1, n_seg)], axis=1)
    all_b = [first_b] + [got_b[k] for k in range(1, n_exp)]
    mine_b = jnp.concatenate([b[:tok] for b in all_b], axis=0)
    meta = jnp.concatenate([b[tok:, :tok] for b in all_b], axis=1)
    xa = {k: hop(mine_a, "expert", k) for k in reversed(range(1, n_exp))}
    xb = {k: hop(mine_b, "seg", k) for k in reversed(range(1, n_seg))}
    xa[0], xb[0] = mine_a, mine_b
    up_2 = fetch(w_up, cut, held_loc, mine_a)

    cb, held = experts_up(
        place, [xa[k] for k in range(n_exp)], [xb[k] for k in range(n_seg)], meta, [*up_1, *up_2], w_up, w_down, topk
    )
    rb = {k: hop(cb[k], "seg", k) for k in reversed(range(1, n_seg))}
    wide = col_b
    outs = []
    part_a = []
    for lo in range(0, col_a, wide):
        ca = experts_down(place, held, w_down, lo, wide, tok, n_exp, n_seg, slice_d)
        ra = {k: hop(ca[k], "expert", k) for k in reversed(range(1, n_exp))}
        sum_a = total_of([ca[0]] + [ra[k] for k in range(1, n_exp)])
        part_a.append([sum_a[:, j * wide:(j + 1) * wide] for j in range(n_seg)])
    sum_b = total_of([cb[0]] + [rb[k] for k in range(1, n_seg)])
    part_b = [sum_b[k * tok:(k + 1) * tok] for k in range(n_exp)]
    fb = {k: hop(part_b[k].astype(jnp.bfloat16), "expert", k) for k in reversed(range(1, n_exp))}
    for part in part_a:
        fa = {j: hop(part[j].astype(jnp.bfloat16), "seg", j) for j in reversed(range(1, n_seg))}
        outs.append(total_of([part[0]] + [fa[j] for j in range(1, n_seg)]))
    outs.append(total_of([part_b[0]] + [fb[k] for k in range(1, n_exp)]))
    return jnp.concatenate(outs, axis=1).astype(jnp.bfloat16)


def plain(tokens, expert_ids, route_weight, w_up, w_down):
    n_exp = lax.axis_size("expert")
    exp_local, width = w_up.shape[:2]
    n_experts = n_exp * exp_local
    topk = expert_ids.shape[1]
    tok_rows, width_seg = tokens.shape
    flat = expert_ids.reshape(-1)
    onehot = (flat[:, None] == jnp.arange(n_experts, dtype=jnp.int32)[None, :]).astype(jnp.int32)
    before = jnp.cumsum(onehot, axis=0) - onehot
    target = flat * SEND_CAP + jnp.sum(before * onehot, axis=1)
    norm_weight = route_weight / jnp.sum(route_weight, axis=1, keepdims=True)
    buffer = jnp.zeros((n_experts * SEND_CAP, width_seg), tokens.dtype)
    packed = buffer.at[target].set(jnp.repeat(tokens, topk, axis=0))
    packed = packed.reshape(n_exp, exp_local * SEND_CAP, width_seg)
    arrived = lax.all_to_all(packed, "expert", split_axis=0, concat_axis=0, tiled=True)
    piece = lax.all_gather(arrived, "seg", axis=2, tiled=True)
    block = piece.reshape(n_exp, exp_local, SEND_CAP, width)
    up_sum = jnp.einsum("sekd,edf->eskf", block, w_up, preferred_element_type=jnp.float32)
    hidden = jax.nn.silu(up_sum).astype(jnp.bfloat16)
    partial_out = jnp.einsum("eskf,efd->sekd", hidden, w_down, preferred_element_type=jnp.float32)
    partial_out = partial_out.reshape(n_exp, exp_local * SEND_CAP, width)
    returned = lax.all_to_all(partial_out, "expert", split_axis=0, concat_axis=0, tiled=True)
    picked = returned.reshape(n_experts * SEND_CAP, width)[target]
    weighted = (picked * norm_weight.reshape(-1)[:, None]).reshape(tok_rows, topk, width).sum(axis=1)
    return lax.psum_scatter(weighted, "seg", scatter_dimension=1, tiled=True).astype(jnp.bfloat16)


def shards(tokens, expert_ids, route_weight, w_up, w_down):
    if tokens.shape[1] % (3 * LANES):
        return plain(tokens, expert_ids, route_weight, w_up, w_down)
    return staged(tokens, expert_ids, route_weight, w_up, w_down)


def solution(mesh):
    placed = (
        P(("dp", "expert"), "seg"),
        P(("dp", "expert"), None),
        P(("dp", "expert"), None),
        P("expert", None, "seg"),
        P("expert", "seg", None),
    )
    return jax.shard_map(
        shards, mesh=mesh, in_specs=placed, out_specs=P(("dp", "expert"), "seg"), check_vma=False
    )
```

```python
import functools

import jax
import jax.numpy as jnp
from jax import lax
from jax.experimental import pallas as pl
from jax.experimental.pallas import tpu as pltpu
from jax.sharding import PartitionSpec as P


SEND_CAP = 21
LANES = 128


def hop(value, axis, k):
    n = lax.axis_size(axis)
    return lax.ppermute(value, axis, [(i, i ^ k) for i in range(n)])


def up_to(value, multiple):
    return -(-value // multiple) * multiple


def call(body, ins, outs, scratch, limit, flops=0, moved=0):
    return pl.pallas_call(
        body,
        in_specs=[pl.BlockSpec(memory_space=space) for _, space in ins],
        out_specs=[pl.BlockSpec(memory_space=pltpu.VMEM) for _ in outs],
        out_shape=outs,
        scratch_shapes=scratch,
        compiler_params=pltpu.CompilerParams(vmem_limit_bytes=limit << 20),
        cost_estimate=pl.CostEstimate(flops=flops, bytes_accessed=moved, transcendentals=0),
    )(*[value for value, _ in ins])


def first_kernel(topk, place, tokens, ids, route, out, ids_v, route_v, sem):
    tok, slice_d = tokens.shape
    copies = [
        pltpu.make_async_copy(ids, ids_v, sem.at[0]),
        pltpu.make_async_copy(route, route_v, sem.at[1]),
        pltpu.make_async_copy(tokens, out.at[pl.ds(0, tok)], sem.at[2]),
    ]
    for copy in copies:
        copy.start()
    for copy in copies:
        copy.wait()
    weight = route_v[...]
    norm = weight / jnp.sum(weight, axis=0, keepdims=True)
    high = norm.astype(jnp.bfloat16).astype(jnp.float32)
    info = jnp.concatenate([ids_v[...].astype(jnp.float32), high, norm - high], axis=0)
    rows = out.shape[0] - tok
    info = jnp.concatenate([info, jnp.zeros((rows - 3 * topk, tok), jnp.float32)], axis=0)
    info = jnp.concatenate([info, jnp.zeros((rows, slice_d - tok), jnp.float32)], axis=1)
    out[tok:, :] = info.astype(jnp.bfloat16)


def fetch_kernel(lo, w_ref, after, *refs):
    outs, sem = refs[:-1], refs[-1]
    copies = [
        pltpu.make_async_copy(w_ref.at[lo + i], out, sem.at[i]) for i, out in enumerate(outs)
    ]
    for copy in copies:
        copy.start()
    for copy in copies:
        copy.wait()


def fetch(w, lo, hi, after):
    return call(
        functools.partial(fetch_kernel, lo),
        [(w, pltpu.HBM), (after, pltpu.HBM)], [pltpu.VMEM(w.shape[1:], w.dtype)] * (hi - lo),
        [pltpu.SemaphoreType.DMA((hi - lo,))], 20, moved=2 * w[0].size * (hi - lo),
    )


def route_rows(meta, n_loc, rows, topk, first_expert, pick, pick_t, row_w):
    tokens = pick.shape[1]
    info = meta[...].astype(jnp.float32)
    ids = info[:topk]
    weights = info[topk:2 * topk] + info[2 * topk:3 * topk]
    earlier = (
        lax.broadcasted_iota(jnp.int32, (tokens, tokens), 0)
        < lax.broadcasted_iota(jnp.int32, (tokens, tokens), 1)
    ).astype(jnp.float32).astype(jnp.bfloat16)
    slot_of_row = lax.broadcasted_iota(jnp.int32, (rows, tokens), 0).astype(jnp.float32)
    for e in range(n_loc):
        here = (ids == (first_expert + e).astype(jnp.float32)).astype(jnp.float32)
        mask = jnp.sum(here, axis=0, keepdims=True)
        gain = jnp.sum(here * weights, axis=0, keepdims=True)
        before = jnp.dot(
            jnp.broadcast_to(mask, (16, tokens)).astype(jnp.bfloat16), earlier,
            preferred_element_type=jnp.float32,
        )
        chosen = jnp.where((slot_of_row == before[:1]) & (mask > 0.5), 1.0, 0.0)
        pick[e * rows:(e + 1) * rows, :] = chosen.astype(jnp.bfloat16)
        row_w[e * rows:(e + 1) * rows, :] = jnp.sum(chosen * gain, axis=1, keepdims=True)
    pick_t[...] = jnp.transpose(pick[...].astype(jnp.float32)).astype(jnp.bfloat16)


def down_loop(first, count, slice_d, rows, place, hidden, pick_t, row_w, w_down, write, scratch):
    buf, sem, high, low = scratch
    deep = buf.shape[0]
    n_loc = w_down.shape[0]
    tiles = count * n_loc

    def tile(t):
        slot = lax.rem(t, deep)
        at = (place[0] ^ (first + lax.div(t, n_loc))) * slice_d
        return pltpu.make_async_copy(
            w_down.at[lax.rem(t, n_loc), :, pl.ds(pl.multiple_of(at, LANES), slice_d)],
            buf.at[slot], sem.at[slot],
        )

    def begin():
        for t in range(min(deep, tiles)):
            tile(jnp.int32(t)).start()

    def body(t, carry):
        tile(t).wait()
        e = lax.rem(t, n_loc)
        at = pl.ds(pl.multiple_of(e * rows, 16), rows)
        result = jnp.dot(hidden[at, :], buf[lax.rem(t, deep)], preferred_element_type=jnp.float32)

        @pl.when(t + deep < tiles)
        def _():
            tile(t + deep).start()

        result = result * row_w[at, :]
        upper = result.astype(jnp.bfloat16)
        high[at, :] = upper
        low[at, :] = (result - upper.astype(jnp.float32)).astype(jnp.bfloat16)

        @pl.when(e == n_loc - 1)
        def _():
            total = jnp.dot(pick_t[...], high[...], preferred_element_type=jnp.float32)
            total = total + jnp.dot(pick_t[...], low[...], preferred_element_type=jnp.float32)
            write(lax.div(t, n_loc), total)

        return carry

    return begin, lambda: lax.fori_loop(0, tiles, body, 0)


def up_kernel(sizes, place, *refs):
    n_exp, n_seg, n_loc, rows, tok, slice_d, tile_f, topk, n_held = sizes
    far = n_seg - 2
    near, refs = refs[:2], refs[2:]
    blocks, refs = refs[:n_exp], refs[n_exp:]
    meta, refs = refs[0], refs[1:]
    w_held, refs = refs[:n_held], refs[n_held:]
    (w_up, w_down), refs = refs[:2], refs[2:]
    outs, refs = refs[:n_exp], refs[n_exp:]
    hidden, pick_t, row_w, pick, joined, packed, buf_u, sem_u = refs[:8]
    per = w_up.shape[2] // tile_f
    tiles = (n_loc - n_held) * per
    deep_u = buf_u.shape[0]

    def tile_u(t):
        cols = pl.ds(pl.multiple_of(lax.rem(t, per) * tile_f, LANES), tile_f)
        slot = lax.rem(t, deep_u)
        return pltpu.make_async_copy(
            w_up.at[n_held + lax.div(t, per), :, cols], buf_u.at[slot], sem_u.at[slot]
        )

    def write(j, total):
        total = total.astype(jnp.bfloat16)
        cols = pl.ds(pl.multiple_of(j * slice_d, LANES), slice_d)
        for k, out in enumerate(outs):
            out[:, cols] = total[k * tok:(k + 1) * tok]

    begin_down, run_down = down_loop(
        2, far, slice_d, rows, place, hidden, pick_t, row_w, w_down, write, refs[8:]
    )
    for t in range(min(deep_u, tiles)):
        tile_u(jnp.int32(t)).start()
    begin_down()
    for k in range(n_exp):
        joined[k * tok:(k + 1) * tok, :] = blocks[k][...]
    route_rows(meta, n_loc, rows, topk, place[1] * n_loc, pick, pick_t, row_w)
    for j in range(n_seg):
        x = near[j][...] if j < 2 else joined[:, (j - 2) * slice_d:(j - 1) * slice_d]
        part = jnp.dot(pick[...], x, preferred_element_type=jnp.float32)
        at = pl.multiple_of((place[0] ^ j) * slice_d, LANES)
        packed[:, pl.ds(at, slice_d)] = part.astype(jnp.bfloat16)

    def up(at, f, weight):
        value = jnp.dot(packed[at, :], weight, preferred_element_type=jnp.float32)
        value = value / (1.0 + jnp.exp(-value))
        cols = pl.ds(pl.multiple_of(f * tile_f, LANES), tile_f)
        hidden[at, cols] = value.astype(jnp.bfloat16)

    for e, held in enumerate(w_held):
        def from_held(f, carry, e=e, held=held):
            cols = pl.ds(pl.multiple_of(f * tile_f, LANES), tile_f)
            up(slice(e * rows, (e + 1) * rows), f, held[:, cols])
            return carry

        lax.fori_loop(0, per, from_held, 0)

    def from_ring(t, carry):
        tile_u(t).wait()
        at = pl.ds(pl.multiple_of((n_held + lax.div(t, per)) * rows, 16), rows)
        up(at, lax.rem(t, per), buf_u[lax.rem(t, deep_u)])

        @pl.when(t + deep_u < tiles)
        def _():
            tile_u(t + deep_u).start()

        return carry

    lax.fori_loop(0, tiles, from_ring, 0)
    run_down()


def down_kernel(j, rows, place, hidden, pick_t, row_w, w_down, out, *scratch):
    def write(_, total):
        out[...] = total.astype(out.dtype)

    begin, run = down_loop(
        j, 1, out.shape[1], rows, place, hidden, pick_t, row_w, w_down, write, scratch
    )
    begin()
    run()


def down_scratch(n_loc, rows, ff, slice_d, deep):
    bf16 = jnp.bfloat16
    return [
        pltpu.VMEM((deep, ff, slice_d), bf16), pltpu.SemaphoreType.DMA((deep,)),
        pltpu.VMEM((n_loc * rows, slice_d), bf16), pltpu.VMEM((n_loc * rows, slice_d), bf16),
    ]


def experts_up(place, near, blocks, meta, w_held, w_up, w_down, topk):
    n_exp, n_seg = len(blocks), lax.axis_size("seg")
    n_loc, ff, width = w_down.shape
    tok = blocks[0].shape[0]
    tokens, slice_d = near[0].shape
    rows = up_to(SEND_CAP * n_exp, 16)
    tile_f = ff // 3
    sizes = (n_exp, n_seg, n_loc, rows, tok, slice_d, tile_f, topk, len(w_held))
    bf16 = jnp.bfloat16
    vmem = lambda values: [(value, pltpu.VMEM) for value in values]
    outs = call(
        functools.partial(up_kernel, sizes),
        [(place, pltpu.SMEM)] + vmem(near) + vmem(blocks) + vmem([meta]) + vmem(w_held)
        + [(w_up, pltpu.HBM), (w_down, pltpu.HBM)],
        [jax.ShapeDtypeStruct(blocks[0].shape, bf16)] * n_exp
        + [jax.ShapeDtypeStruct((n_loc * rows, ff), bf16),
           jax.ShapeDtypeStruct((tokens, n_loc * rows), bf16),
           jax.ShapeDtypeStruct((n_loc * rows, 1), jnp.float32)],
        [pltpu.VMEM((n_loc * rows, tokens), bf16),
         pltpu.VMEM((tokens, blocks[0].shape[1]), bf16),
         pltpu.VMEM((n_loc * rows, width), bf16),
         pltpu.VMEM((3, width, tile_f), bf16),
         pltpu.SemaphoreType.DMA((3,))] + down_scratch(n_loc, rows, ff, slice_d, 4),
        26, flops=2 * n_loc * 256 * width * ff, moved=n_loc * ff * width * 2,
    )
    return outs[:n_exp], outs[n_exp:]


def experts_down(place, held, w_down, j, slice_d, dtype):
    n_loc, ff, _ = w_down.shape
    hidden, pick_t, row_w = held
    rows = hidden.shape[0] // n_loc
    return call(
        functools.partial(down_kernel, j, rows),
        [(place, pltpu.SMEM), (hidden, pltpu.VMEM), (pick_t, pltpu.VMEM), (row_w, pltpu.VMEM),
         (w_down, pltpu.HBM)],
        [jax.ShapeDtypeStruct((pick_t.shape[0], slice_d), dtype)],
        down_scratch(n_loc, rows, ff, slice_d, 4),
        20, flops=2 * n_loc * 256 * slice_d * ff, moved=2 * n_loc * ff * slice_d,
    )[0]


def total_of(parts):
    total = parts[0].astype(jnp.float32)
    for part in parts[1:]:
        total = total + part.astype(jnp.float32)
    return total


def staged(tokens, expert_ids, route_weight, w_up, w_down):
    n_exp = lax.axis_size("expert")
    n_seg = lax.axis_size("seg")
    tok, slice_d = tokens.shape
    topk = expert_ids.shape[1]
    far = range(2, n_seg)
    peers = range(1, n_exp)
    place = jnp.stack([lax.axis_index("seg"), lax.axis_index("expert")]).astype(jnp.int32)

    a = [hop(tokens, "seg", k) for k in far]
    rows = tok + up_to(3 * topk, 16)
    first = call(
        functools.partial(first_kernel, topk),
        [(place, pltpu.SMEM), (tokens, pltpu.HBM), (expert_ids.T, pltpu.HBM),
         (route_weight.T, pltpu.HBM)],
        [jax.ShapeDtypeStruct((rows, slice_d), tokens.dtype)],
        [pltpu.VMEM((topk, tok), jnp.int32), pltpu.VMEM((topk, tok), jnp.float32),
         pltpu.SemaphoreType.DMA((3,))], 62,
    )[0]
    b = [first] + [hop(first, "expert", k) for k in peers]
    near = jnp.concatenate([x[:tok] for x in b], axis=0)
    e = hop(near, "seg", 1)
    block = jnp.concatenate(a, axis=1)
    blocks = [block] + [hop(block, "expert", k) for k in peers]
    w_held = fetch(w_up, 0, w_up.shape[0] // 2, block)
    meta = jnp.concatenate([x[tok:, :tok] for x in b], axis=1)

    c, held = experts_up(place, [near, e], blocks, meta, w_held, w_up, w_down, topk)
    c = [c[0]] + [hop(c[k], "expert", k) for k in peers]
    g = hop(experts_down(place, held, w_down, 1, slice_d, jnp.bfloat16), "seg", 1)
    own = experts_down(place, held, w_down, 0, slice_d, jnp.float32)
    total = total_of(c).astype(jnp.bfloat16)
    sent = [total[:, (k - 2) * slice_d:(k - 1) * slice_d] for k in far]
    d = [hop(x, "seg", k) for x, k in zip(sent, far)]
    own = total_of([own, g])
    mine = own[:tok]
    own = own.astype(jnp.bfloat16)
    h = [hop(own[k * tok:(k + 1) * tok], "expert", k) for k in peers]
    return total_of([mine] + h + d).astype(jnp.bfloat16)


def plain(tokens, expert_ids, route_weight, w_up, w_down):
    n_exp = lax.axis_size("expert")
    exp_local, width = w_up.shape[:2]
    n_experts = n_exp * exp_local
    topk = expert_ids.shape[1]
    tok_rows, width_seg = tokens.shape
    flat = expert_ids.reshape(-1)
    onehot = (flat[:, None] == jnp.arange(n_experts, dtype=jnp.int32)[None, :]).astype(jnp.int32)
    before = jnp.cumsum(onehot, axis=0) - onehot
    target = flat * SEND_CAP + jnp.sum(before * onehot, axis=1)
    norm_weight = route_weight / jnp.sum(route_weight, axis=1, keepdims=True)
    buffer = jnp.zeros((n_experts * SEND_CAP, width_seg), tokens.dtype)
    packed = buffer.at[target].set(jnp.repeat(tokens, topk, axis=0))
    packed = packed.reshape(n_exp, exp_local * SEND_CAP, width_seg)
    arrived = lax.all_to_all(packed, "expert", split_axis=0, concat_axis=0, tiled=True)
    piece = lax.all_gather(arrived, "seg", axis=2, tiled=True)
    block = piece.reshape(n_exp, exp_local, SEND_CAP, width)
    up_sum = jnp.einsum("sekd,edf->eskf", block, w_up, preferred_element_type=jnp.float32)
    hidden = jax.nn.silu(up_sum).astype(jnp.bfloat16)
    partial_out = jnp.einsum("eskf,efd->sekd", hidden, w_down, preferred_element_type=jnp.float32)
    partial_out = partial_out.reshape(n_exp, exp_local * SEND_CAP, width)
    returned = lax.all_to_all(partial_out, "expert", split_axis=0, concat_axis=0, tiled=True)
    picked = returned.reshape(n_experts * SEND_CAP, width)[target]
    weighted = (picked * norm_weight.reshape(-1)[:, None]).reshape(tok_rows, topk, width).sum(axis=1)
    return lax.psum_scatter(weighted, "seg", scatter_dimension=1, tiled=True).astype(jnp.bfloat16)


def shards(tokens, expert_ids, route_weight, w_up, w_down):
    if tokens.shape[1] % LANES:
        return plain(tokens, expert_ids, route_weight, w_up, w_down)
    return staged(tokens, expert_ids, route_weight, w_up, w_down)


def solution(mesh):
    placed = (
        P(("dp", "expert"), "seg"),
        P(("dp", "expert"), None),
        P(("dp", "expert"), None),
        P("expert", None, "seg"),
        P("expert", "seg", None),
    )
    return jax.shard_map(
        shards, mesh=mesh, in_specs=placed, out_specs=P(("dp", "expert"), "seg"), check_vma=False
    )
```

```python
import functools

import jax
import jax.numpy as jnp
from jax import lax
from jax.experimental import pallas as pl
from jax.experimental.pallas import tpu as pltpu
from jax.sharding import PartitionSpec as P


SEND_CAP = 21
LANES = 128


def hop(value, axis, k):
    n = lax.axis_size(axis)
    return lax.ppermute(value, axis, [(i, i ^ k) for i in range(n)])


def up_to(value, multiple):
    return -(-value // multiple) * multiple


def call(body, ins, outs, scratch, limit, flops=0, moved=0, aliases=()):
    return pl.pallas_call(
        body,
        in_specs=[pl.BlockSpec(memory_space=space) for _, space in ins],
        out_specs=[pl.BlockSpec(memory_space=pltpu.VMEM) for _ in outs],
        out_shape=outs,
        scratch_shapes=scratch,
        input_output_aliases=dict(aliases),
        compiler_params=pltpu.CompilerParams(vmem_limit_bytes=limit << 20),
        cost_estimate=pl.CostEstimate(flops=flops, bytes_accessed=moved, transcendentals=0),
    )(*[value for value, _ in ins])


def route_kernel(topk, place, ids, route, w_up, out, weights, sem):
    copy = pltpu.make_async_copy(w_up.at[0], weights, sem)
    copy.start()
    tok = ids.shape[1]
    rows = up_to(3 * topk, 16)
    weight = route[...]
    norm = weight / jnp.sum(weight, axis=0, keepdims=True)
    high = norm.astype(jnp.bfloat16).astype(jnp.float32)
    info = jnp.concatenate([ids[...].astype(jnp.float32), high, norm - high], axis=0)
    info = jnp.concatenate([info, jnp.zeros((rows - 3 * topk, tok), jnp.float32)], axis=0)
    info = jnp.concatenate([info, jnp.zeros((rows, out.shape[1] - tok), jnp.float32)], axis=1)
    out[...] = jnp.zeros(out.shape, out.dtype)
    out[:rows, :] = info.astype(jnp.bfloat16)
    copy.wait()


def fetch_kernel(lo, w_ref, after, place, *refs):
    outs, sem = refs[:-1], refs[-1]
    copies = [
        pltpu.make_async_copy(w_ref.at[lo + i], out, sem.at[i]) for i, out in enumerate(outs)
    ]
    for copy in copies:
        copy.start()
    for copy in copies:
        copy.wait()


def fetch(w, lo, hi, after, place):
    return call(
        functools.partial(fetch_kernel, lo),
        [(w, pltpu.HBM), (after, pltpu.HBM), (place, pltpu.SMEM)], [pltpu.VMEM(w.shape[1:], w.dtype)] * (hi - lo),
        [pltpu.SemaphoreType.DMA((hi - lo,))], 20, moved=2 * w[0].size * (hi - lo),
    )


def route_rows(info, n_loc, rows, topk, first_expert, pick, pick_t, row_w):
    tokens = pick.shape[1]
    info = info.astype(jnp.float32)
    ids = info[:topk]
    weights = info[topk:2 * topk] + info[2 * topk:3 * topk]
    earlier = (
        lax.broadcasted_iota(jnp.int32, (tokens, tokens), 0)
        < lax.broadcasted_iota(jnp.int32, (tokens, tokens), 1)
    ).astype(jnp.float32).astype(jnp.bfloat16)
    slot_of_row = lax.broadcasted_iota(jnp.int32, (rows, tokens), 0).astype(jnp.float32)
    for e in range(n_loc):
        here = (ids == (first_expert + e).astype(jnp.float32)).astype(jnp.float32)
        mask = jnp.sum(here, axis=0, keepdims=True)
        gain = jnp.sum(here * weights, axis=0, keepdims=True)
        before = jnp.dot(
            jnp.broadcast_to(mask, (16, tokens)).astype(jnp.bfloat16), earlier,
            preferred_element_type=jnp.float32,
        )
        chosen = jnp.where((slot_of_row == before[:1]) & (mask > 0.5), 1.0, 0.0)
        pick[e * rows:(e + 1) * rows, :] = chosen.astype(jnp.bfloat16)
        row_w[e * rows:(e + 1) * rows, :] = jnp.sum(chosen * gain, axis=1, keepdims=True)
    pick_t[...] = jnp.transpose(pick[...].astype(jnp.float32)).astype(jnp.bfloat16)


def piece(e, ff, slice_d):
    per = ff // slice_d
    return slice(e // per * ff, (e // per + 1) * ff), slice(e % per * slice_d, (e % per + 1) * slice_d)


def slice_copies(place, j, slice_d, w_down, ahead, sem):
    n_loc, ff, _ = w_down.shape
    at = pl.multiple_of((place[0] ^ j) * slice_d, LANES)
    return [
        pltpu.make_async_copy(
            w_down.at[e, :, pl.ds(at, slice_d)], ahead.at[piece(e, ff, slice_d)], sem.at[e]
        )
        for e in range(n_loc)
    ]


def down_rows(hidden, weight, row_w, at, high, low):
    result = jnp.dot(hidden[at, :], weight, preferred_element_type=jnp.float32)
    result = result * row_w[at, :]
    upper = result.astype(jnp.bfloat16)
    high[at, :] = upper
    low[at, :] = (result - upper.astype(jnp.float32)).astype(jnp.bfloat16)


def combine(pick_t, high, low):
    total = jnp.dot(pick_t[...], high[...], preferred_element_type=jnp.float32)
    return total + jnp.dot(pick_t[...], low[...], preferred_element_type=jnp.float32)


def down_slice(weights, hidden, pick_t, row_w, rows, n_loc, slice_d, high, low):
    for e in range(n_loc):
        at = slice(e * rows, (e + 1) * rows)
        weight = weights[piece(e, hidden.shape[1], slice_d)]
        down_rows(hidden, weight, row_w, at, high, low)
    return combine(pick_t, high, low)


def up_kernel(sizes, place, *refs):
    n_exp, n_seg, n_loc, rows, tok, slice_d, tile_f, topk, n_held = sizes
    far = n_seg - 2
    near, refs = refs[:2], refs[2:]
    blocks, refs = refs[:n_exp], refs[n_exp:]
    w_held, refs = refs[:n_held], refs[n_held:]
    (w_up, w_down), refs = refs[:2], refs[2:]
    outs, refs = refs[:n_exp], refs[n_exp:]
    (hidden, pick_t, row_w), room, refs = refs[:3], refs[3:3 + n_held], refs[3 + n_held:]
    pick, joined, packed, buf_u, sem_u, sem_a, high, low = refs
    per = w_up.shape[2] // tile_f
    tiles = (n_loc - n_held) * per
    deep_u = buf_u.shape[0]

    def tile_u(t):
        cols = pl.ds(pl.multiple_of(lax.rem(t, per) * tile_f, LANES), tile_f)
        slot = lax.rem(t, deep_u)
        return pltpu.make_async_copy(
            w_up.at[n_held + lax.div(t, per), :, cols], buf_u.at[slot], sem_u.at[slot]
        )

    for t in range(min(deep_u, tiles)):
        tile_u(jnp.int32(t)).start()
    wide = far * slice_d
    for k in range(n_exp):
        joined[k * tok:(k + 1) * tok, :] = blocks[k][:, :wide]
    info = jnp.concatenate([x[:up_to(3 * topk, 16), wide:wide + tok] for x in blocks], axis=1)
    route_rows(info, n_loc, rows, topk, place[1] * n_loc, pick, pick_t, row_w)
    for j in range(n_seg):
        x = near[j][...] if j < 2 else joined[:, (j - 2) * slice_d:(j - 1) * slice_d]
        part = jnp.dot(pick[...], x, preferred_element_type=jnp.float32)
        at = pl.multiple_of((place[0] ^ j) * slice_d, LANES)
        packed[:, pl.ds(at, slice_d)] = part.astype(jnp.bfloat16)

    def up(at, f, weight):
        value = jnp.dot(packed[at, :], weight, preferred_element_type=jnp.float32)
        value = value / (1.0 + jnp.exp(-value))
        cols = pl.ds(pl.multiple_of(f * tile_f, LANES), tile_f)
        hidden[at, cols] = value.astype(jnp.bfloat16)

    slices = list(range(2, n_seg)) + [1]
    copies = [
        slice_copies(place, j, slice_d, w_down, room[i], sem_a.at[i]) for i, j in enumerate(slices)
    ]
    for e, held in enumerate(w_held):
        def from_held(f, carry, e=e, held=held):
            cols = pl.ds(pl.multiple_of(f * tile_f, LANES), tile_f)
            up(slice(e * rows, (e + 1) * rows), f, held[:, cols])
            return carry

        lax.fori_loop(0, per, from_held, 0)
        for copy in copies[e]:
            copy.start()

    def from_ring(t, carry):
        tile_u(t).wait()
        at = pl.ds(pl.multiple_of((n_held + lax.div(t, per)) * rows, 16), rows)
        up(at, lax.rem(t, per), buf_u[lax.rem(t, deep_u)])

        @pl.when(t + deep_u < tiles)
        def _():
            tile_u(t + deep_u).start()

        return carry

    lax.fori_loop(0, tiles, from_ring, 0)
    for i in range(far):
        for copy in copies[i]:
            copy.wait()
        total = down_slice(room[i], hidden, pick_t, row_w, rows, n_loc, slice_d, high, low)
        total = total.astype(jnp.bfloat16)
        for k, out in enumerate(outs):
            out[:, i * slice_d:(i + 1) * slice_d] = total[k * tok:(k + 1) * tok]
    for copy in copies[far]:
        copy.wait()


def down_kernel(rows, n_loc, hidden, pick_t, row_w, weights, out, high, low):
    total = down_slice(weights, hidden, pick_t, row_w, rows, n_loc, out.shape[1], high, low)
    out[...] = total.astype(out.dtype)


def own_kernel(rows, place, hidden, pick_t, row_w, w_down, out, buf, sem, high, low):
    n_loc = w_down.shape[0]
    at = pl.multiple_of(place[0] * out.shape[1], LANES)
    copies = [
        pltpu.make_async_copy(w_down.at[e, :, pl.ds(at, out.shape[1])], buf.at[e], sem.at[e])
        for e in range(n_loc)
    ]
    for copy in copies:
        copy.start()
    for e, copy in enumerate(copies):
        copy.wait()
        down_rows(hidden, buf[e], row_w, slice(e * rows, (e + 1) * rows), high, low)
    out[...] = combine(pick_t, high, low).astype(out.dtype)


def down_scratch(n_loc, rows, ff, slice_d, deep):
    bf16 = jnp.bfloat16
    return [
        pltpu.VMEM((deep, ff, slice_d), bf16), pltpu.SemaphoreType.DMA((deep,)),
        pltpu.VMEM((n_loc * rows, slice_d), bf16), pltpu.VMEM((n_loc * rows, slice_d), bf16),
    ]


def experts_up(place, near, blocks, w_held, w_up, w_down, topk):
    n_exp, n_seg = len(blocks), lax.axis_size("seg")
    n_loc, ff, width = w_down.shape
    tok = blocks[0].shape[0]
    tokens, slice_d = near[0].shape
    rows = up_to(SEND_CAP * n_exp, 16)
    tile_f = ff // 3
    wide = (n_seg - 2) * slice_d
    sizes = (n_exp, n_seg, n_loc, rows, tok, slice_d, tile_f, topk, len(w_held))
    bf16 = jnp.bfloat16
    vmem = lambda values: [(value, pltpu.VMEM) for value in values]
    outs = call(
        functools.partial(up_kernel, sizes),
        [(place, pltpu.SMEM)] + vmem(near) + vmem(blocks) + vmem(w_held)
        + [(w_up, pltpu.HBM), (w_down, pltpu.HBM)],
        [jax.ShapeDtypeStruct((tok, wide), bf16)] * n_exp
        + [jax.ShapeDtypeStruct((n_loc * rows, ff), bf16),
           jax.ShapeDtypeStruct((tokens, n_loc * rows), bf16),
           jax.ShapeDtypeStruct((n_loc * rows, 1), jnp.float32)]
        + [pltpu.VMEM(w.shape, bf16) for w in w_held],
        [pltpu.VMEM((n_loc * rows, tokens), bf16),
         pltpu.VMEM((tokens, wide), bf16),
         pltpu.VMEM((n_loc * rows, width), bf16),
         pltpu.VMEM((3, width, tile_f), bf16),
         pltpu.SemaphoreType.DMA((3,)),
         pltpu.SemaphoreType.DMA((len(w_held), n_loc)),
         pltpu.VMEM((n_loc * rows, slice_d), bf16), pltpu.VMEM((n_loc * rows, slice_d), bf16)],
        15, flops=2 * n_loc * 256 * width * ff, moved=n_loc * ff * width * 2,
        aliases=[(3 + n_exp + i, n_exp + 3 + i) for i in range(len(w_held))],
    )
    return outs[:n_exp], outs[n_exp:n_exp + 3], outs[n_exp + 3:]


def experts_down(held, weights, n_loc, slice_d, dtype):
    hidden, pick_t, row_w = held
    rows, ff = hidden.shape[0] // n_loc, hidden.shape[1]
    bf16 = jnp.bfloat16
    return call(
        functools.partial(down_kernel, rows, n_loc),
        [(x, pltpu.VMEM) for x in (hidden, pick_t, row_w, weights)],
        [jax.ShapeDtypeStruct((pick_t.shape[0], slice_d), dtype)],
        [pltpu.VMEM((n_loc * rows, slice_d), bf16), pltpu.VMEM((n_loc * rows, slice_d), bf16)],
        16, flops=2 * n_loc * 256 * slice_d * ff,
    )[0]


def experts_own(place, held, w_down, slice_d):
    hidden, pick_t, row_w = held
    n_loc, ff, _ = w_down.shape
    rows = hidden.shape[0] // n_loc
    return call(
        functools.partial(own_kernel, rows),
        [(place, pltpu.SMEM)] + [(x, pltpu.VMEM) for x in (hidden, pick_t, row_w)]
        + [(w_down, pltpu.HBM)],
        [jax.ShapeDtypeStruct((pick_t.shape[0], slice_d), jnp.float32)],
        down_scratch(n_loc, rows, ff, slice_d, n_loc),
        16, flops=2 * n_loc * 256 * slice_d * ff, moved=2 * n_loc * ff * slice_d,
    )[0]


def total_of(parts):
    total = parts[0].astype(jnp.float32)
    for part in parts[1:]:
        total = total + part.astype(jnp.float32)
    return total


def staged(tokens, expert_ids, route_weight, w_up, w_down):
    n_exp = lax.axis_size("expert")
    n_seg = lax.axis_size("seg")
    tok, slice_d = tokens.shape
    topk = expert_ids.shape[1]
    far = range(2, n_seg)
    peers = range(1, n_exp)
    place = jnp.stack([lax.axis_index("seg"), lax.axis_index("expert")]).astype(jnp.int32)

    a = [hop(tokens, "seg", k) for k in far]
    b = [tokens] + [hop(tokens, "expert", k) for k in peers]
    route, held_0 = call(
        functools.partial(route_kernel, topk),
        [(place, pltpu.SMEM), (expert_ids.T, pltpu.VMEM), (route_weight.T, pltpu.VMEM),
         (w_up, pltpu.HBM)],
        [jax.ShapeDtypeStruct((tok, LANES), tokens.dtype), pltpu.VMEM(w_up.shape[1:], w_up.dtype)],
        [pltpu.SemaphoreType.DMA], 20,
    )
    near = jnp.concatenate(b, axis=0)
    e = hop(near, "seg", 1)
    block = jnp.concatenate(a + [route], axis=1)
    blocks = [block] + [hop(block, "expert", k) for k in peers]
    w_held = [held_0, *fetch(w_up, 1, n_seg - 1, block, place)]

    c, held, ahead = experts_up(place, [near, e], blocks, w_held, w_up, w_down, topk)
    c = [c[0]] + [hop(c[k], "expert", k) for k in peers]
    n_loc = w_up.shape[0]
    g = hop(experts_down(held, ahead[-1], n_loc, slice_d, jnp.bfloat16), "seg", 1)
    own = experts_own(place, held, w_down, slice_d)
    total = total_of(c).astype(jnp.bfloat16)
    sent = [total[:, (k - 2) * slice_d:(k - 1) * slice_d] for k in far]
    d = [hop(x, "seg", k) for x, k in zip(sent, far)]
    own = total_of([own, g])
    mine = own[:tok]
    own = own.astype(jnp.bfloat16)
    h = [hop(own[k * tok:(k + 1) * tok], "expert", k) for k in peers]
    return total_of([mine] + h + d).astype(jnp.bfloat16)


def plain(tokens, expert_ids, route_weight, w_up, w_down):
    n_exp = lax.axis_size("expert")
    exp_local, width = w_up.shape[:2]
    n_experts = n_exp * exp_local
    topk = expert_ids.shape[1]
    tok_rows, width_seg = tokens.shape
    flat = expert_ids.reshape(-1)
    onehot = (flat[:, None] == jnp.arange(n_experts, dtype=jnp.int32)[None, :]).astype(jnp.int32)
    before = jnp.cumsum(onehot, axis=0) - onehot
    target = flat * SEND_CAP + jnp.sum(before * onehot, axis=1)
    norm_weight = route_weight / jnp.sum(route_weight, axis=1, keepdims=True)
    buffer = jnp.zeros((n_experts * SEND_CAP, width_seg), tokens.dtype)
    packed = buffer.at[target].set(jnp.repeat(tokens, topk, axis=0))
    packed = packed.reshape(n_exp, exp_local * SEND_CAP, width_seg)
    arrived = lax.all_to_all(packed, "expert", split_axis=0, concat_axis=0, tiled=True)
    piece = lax.all_gather(arrived, "seg", axis=2, tiled=True)
    block = piece.reshape(n_exp, exp_local, SEND_CAP, width)
    up_sum = jnp.einsum("sekd,edf->eskf", block, w_up, preferred_element_type=jnp.float32)
    hidden = jax.nn.silu(up_sum).astype(jnp.bfloat16)
    partial_out = jnp.einsum("eskf,efd->sekd", hidden, w_down, preferred_element_type=jnp.float32)
    partial_out = partial_out.reshape(n_exp, exp_local * SEND_CAP, width)
    returned = lax.all_to_all(partial_out, "expert", split_axis=0, concat_axis=0, tiled=True)
    picked = returned.reshape(n_experts * SEND_CAP, width)[target]
    weighted = (picked * norm_weight.reshape(-1)[:, None]).reshape(tok_rows, topk, width).sum(axis=1)
    return lax.psum_scatter(weighted, "seg", scatter_dimension=1, tiled=True).astype(jnp.bfloat16)


def shards(tokens, expert_ids, route_weight, w_up, w_down):
    n_exp, n_seg = lax.axis_size("expert"), lax.axis_size("seg")
    n_loc, ff, width = w_down.shape
    slice_d = tokens.shape[1]
    paired = n_exp & (n_exp - 1) == 0 and n_seg & (n_seg - 1) == 0
    room = n_loc >= n_seg > 2 and n_loc * slice_d <= width and ff % (3 * LANES) == 0
    if not (paired and room and slice_d % LANES == 0 and ff % slice_d == 0):
        return plain(tokens, expert_ids, route_weight, w_up, w_down)
    return staged(tokens, expert_ids, route_weight, w_up, w_down)


def solution(mesh):
    placed = (
        P(("dp", "expert"), "seg"),
        P(("dp", "expert"), None),
        P(("dp", "expert"), None),
        P("expert", None, "seg"),
        P("expert", "seg", None),
    )
    return jax.shard_map(
        shards, mesh=mesh, in_specs=placed, out_specs=P(("dp", "expert"), "seg"), check_vma=False
    )
```

```python
import functools

import jax
import jax.numpy as jnp
from jax import lax
from jax.experimental import pallas as pl
from jax.experimental.pallas import tpu as pltpu
from jax.sharding import PartitionSpec as P


SEND_CAP = 21
LANES = 128


def hop(value, axis, k):
    n = lax.axis_size(axis)
    return lax.ppermute(value, axis, [(i, i ^ k) for i in range(n)])


def up_to(value, multiple):
    return -(-value // multiple) * multiple


def call(body, ins, outs, scratch, limit, flops=0, moved=0, aliases=()):
    return pl.pallas_call(
        body,
        in_specs=[pl.BlockSpec(memory_space=space) for _, space in ins],
        out_specs=[pl.BlockSpec(memory_space=pltpu.VMEM) for _ in outs],
        out_shape=outs,
        scratch_shapes=scratch,
        input_output_aliases=dict(aliases),
        compiler_params=pltpu.CompilerParams(vmem_limit_bytes=limit << 20),
        cost_estimate=pl.CostEstimate(flops=flops, bytes_accessed=moved, transcendentals=0),
    )(*[value for value, _ in ins])


def route_kernel(topk, place, routes, w_up, out, weights, sem):
    copy = pltpu.make_async_copy(w_up.at[0], weights, sem)
    copy.start()
    tok = routes.shape[1]
    rows = up_to(3 * topk, 16)
    weight = routes[topk:, :]
    norm = weight / jnp.sum(weight, axis=0, keepdims=True)
    high = norm.astype(jnp.bfloat16).astype(jnp.float32)
    info = jnp.concatenate([routes[:topk, :], high, norm - high], axis=0)
    info = jnp.concatenate([info, jnp.zeros((rows - 3 * topk, tok), jnp.float32)], axis=0)
    info = jnp.concatenate([info, jnp.zeros((rows, out.shape[1] - tok), jnp.float32)], axis=1)
    out[...] = jnp.zeros(out.shape, out.dtype)
    out[:rows, :] = info.astype(jnp.bfloat16)
    copy.wait()


def join_kernel(axis, *refs):
    at = 0
    for x in refs[:-1]:
        size = x.shape[axis]
        if axis:
            refs[-1][:, at:at + size] = x[...]
        else:
            refs[-1][at:at + size, :] = x[...]
        at += size


def join(values, axis):
    shape = list(values[0].shape)
    shape[axis] = sum(x.shape[axis] for x in values)
    return call(
        functools.partial(join_kernel, axis), [(x, pltpu.VMEM) for x in values],
        [jax.ShapeDtypeStruct(tuple(shape), values[0].dtype)], [], 4,
    )[0]


def fetch_kernel(lo, w_ref, after, place, *refs):
    outs, sem = refs[:-1], refs[-1]
    copies = [
        pltpu.make_async_copy(w_ref.at[lo + i], out, sem.at[i]) for i, out in enumerate(outs)
    ]
    for copy in copies:
        copy.start()
    for copy in copies:
        copy.wait()


def fetch(w, lo, hi, after, place):
    return call(
        functools.partial(fetch_kernel, lo),
        [(w, pltpu.HBM), (after, pltpu.HBM), (place, pltpu.SMEM)], [pltpu.VMEM(w.shape[1:], w.dtype)] * (hi - lo),
        [pltpu.SemaphoreType.DMA((hi - lo,))], 20, moved=2 * w[0].size * (hi - lo),
    )


def route_rows(info, n_loc, rows, topk, first_expert, pick, pick_t, row_w):
    tokens = pick.shape[1]
    info = info.astype(jnp.float32)
    ids = info[:topk]
    weights = info[topk:2 * topk] + info[2 * topk:3 * topk]
    earlier = (
        lax.broadcasted_iota(jnp.int32, (tokens, tokens), 0)
        < lax.broadcasted_iota(jnp.int32, (tokens, tokens), 1)
    ).astype(jnp.float32).astype(jnp.bfloat16)
    slot_of_row = lax.broadcasted_iota(jnp.int32, (rows, tokens), 0).astype(jnp.float32)
    for e in range(n_loc):
        here = (ids == (first_expert + e).astype(jnp.float32)).astype(jnp.float32)
        mask = jnp.sum(here, axis=0, keepdims=True)
        gain = jnp.sum(here * weights, axis=0, keepdims=True)
        before = jnp.dot(
            jnp.broadcast_to(mask, (16, tokens)).astype(jnp.bfloat16), earlier,
            preferred_element_type=jnp.float32,
        )
        chosen = jnp.where((slot_of_row == before[:1]) & (mask > 0.5), 1.0, 0.0)
        pick[e * rows:(e + 1) * rows, :] = chosen.astype(jnp.bfloat16)
        row_w[e * rows:(e + 1) * rows, :] = jnp.sum(chosen * gain, axis=1, keepdims=True)
    pick_t[...] = jnp.transpose(pick[...].astype(jnp.float32)).astype(jnp.bfloat16)


def piece(e, ff, slice_d):
    per = ff // slice_d
    return slice(e // per * ff, (e // per + 1) * ff), slice(e % per * slice_d, (e % per + 1) * slice_d)


def slice_copies(place, j, slice_d, w_down, ahead, sem):
    n_loc, ff, _ = w_down.shape
    at = pl.multiple_of((place[0] ^ j) * slice_d, LANES)
    return [
        pltpu.make_async_copy(
            w_down.at[e, :, pl.ds(at, slice_d)], ahead.at[piece(e, ff, slice_d)], sem.at[e]
        )
        for e in range(n_loc)
    ]


def down_rows(hidden, weight, row_w, at, high, low):
    result = jnp.dot(hidden[at, :], weight, preferred_element_type=jnp.float32)
    result = result * row_w[at, :]
    upper = result.astype(jnp.bfloat16)
    high[at, :] = upper
    low[at, :] = (result - upper.astype(jnp.float32)).astype(jnp.bfloat16)


def combine(pick_t, high, low):
    total = jnp.dot(pick_t[...], high[...], preferred_element_type=jnp.float32)
    return total + jnp.dot(pick_t[...], low[...], preferred_element_type=jnp.float32)


def down_slice(weights, hidden, pick_t, row_w, rows, n_loc, slice_d, high, low):
    for e in range(n_loc):
        at = slice(e * rows, (e + 1) * rows)
        weight = weights[piece(e, hidden.shape[1], slice_d)]
        down_rows(hidden, weight, row_w, at, high, low)
    return combine(pick_t, high, low)


def up_kernel(sizes, place, *refs):
    n_exp, n_seg, n_loc, rows, tok, slice_d, tile_f, topk, n_held = sizes
    far = n_seg - 2
    near, refs = refs[:2], refs[2:]
    blocks, refs = refs[:n_exp], refs[n_exp:]
    w_held, refs = refs[:n_held], refs[n_held:]
    (w_up, w_down), refs = refs[:2], refs[2:]
    outs, refs = refs[:n_exp], refs[n_exp:]
    (hidden, pick_t, row_w), room, refs = refs[:3], refs[3:3 + n_held], refs[3 + n_held:]
    pick, joined, packed, buf_u, sem_u, sem_a, high, low = refs
    per = w_up.shape[2] // tile_f
    tiles = (n_loc - n_held) * per
    deep_u = buf_u.shape[0]

    def tile_u(t):
        cols = pl.ds(pl.multiple_of(lax.rem(t, per) * tile_f, LANES), tile_f)
        slot = lax.rem(t, deep_u)
        return pltpu.make_async_copy(
            w_up.at[n_held + lax.div(t, per), :, cols], buf_u.at[slot], sem_u.at[slot]
        )

    for t in range(min(deep_u, tiles)):
        tile_u(jnp.int32(t)).start()
    wide = far * slice_d
    for k in range(n_exp):
        joined[k * tok:(k + 1) * tok, :] = blocks[k][:, :wide]
    info = jnp.concatenate([x[:up_to(3 * topk, 16), wide:wide + tok] for x in blocks], axis=1)
    route_rows(info, n_loc, rows, topk, place[1] * n_loc, pick, pick_t, row_w)
    for j in range(n_seg):
        x = near[j][...] if j < 2 else joined[:, (j - 2) * slice_d:(j - 1) * slice_d]
        part = jnp.dot(pick[...], x, preferred_element_type=jnp.float32)
        at = pl.multiple_of((place[0] ^ j) * slice_d, LANES)
        packed[:, pl.ds(at, slice_d)] = part.astype(jnp.bfloat16)

    def up(at, cols, weight):
        value = jnp.dot(packed[at, :], weight, preferred_element_type=jnp.float32)
        value = value / (1.0 + jnp.exp(-value))
        hidden[at, cols] = value.astype(jnp.bfloat16)

    slices = list(range(2, n_seg)) + [1]
    copies = [
        slice_copies(place, j, slice_d, w_down, room[i], sem_a.at[i]) for i, j in enumerate(slices)
    ]
    for e, held in enumerate(w_held):
        half = held.shape[1] // 2

        def from_held(f, carry, e=e, held=held):
            cols = pl.ds(pl.multiple_of(f * half, LANES), half)
            up(slice(e * rows, (e + 1) * rows), cols, held[:, cols])
            return carry

        lax.fori_loop(0, 2, from_held, 0)
        for copy in copies[e]:
            copy.start()

    def from_ring(t, carry):
        tile_u(t).wait()
        at = pl.ds(pl.multiple_of((n_held + lax.div(t, per)) * rows, 16), rows)
        cols = pl.ds(pl.multiple_of(lax.rem(t, per) * tile_f, LANES), tile_f)
        up(at, cols, buf_u[lax.rem(t, deep_u)])

        @pl.when(t + deep_u < tiles)
        def _():
            tile_u(t + deep_u).start()

        return carry

    lax.fori_loop(0, tiles, from_ring, 0)
    for i in range(far):
        for copy in copies[i]:
            copy.wait()
        total = down_slice(room[i], hidden, pick_t, row_w, rows, n_loc, slice_d, high, low)
        total = total.astype(jnp.bfloat16)
        for k, out in enumerate(outs):
            out[:, i * slice_d:(i + 1) * slice_d] = total[k * tok:(k + 1) * tok]
    for copy in copies[far]:
        copy.wait()


def down_kernel(rows, n_loc, hidden, pick_t, row_w, weights, out, high, low):
    total = down_slice(weights, hidden, pick_t, row_w, rows, n_loc, out.shape[1], high, low)
    out[...] = total.astype(out.dtype)


def own_kernel(rows, place, hidden, pick_t, row_w, w_down, out, buf, sem, high, low):
    n_loc = w_down.shape[0]
    at = pl.multiple_of(place[0] * out.shape[1], LANES)
    copies = [
        pltpu.make_async_copy(w_down.at[e, :, pl.ds(at, out.shape[1])], buf.at[e], sem.at[e])
        for e in range(n_loc)
    ]
    for copy in copies:
        copy.start()
    for e, copy in enumerate(copies):
        copy.wait()
        down_rows(hidden, buf[e], row_w, slice(e * rows, (e + 1) * rows), high, low)
    out[...] = combine(pick_t, high, low).astype(out.dtype)


def down_scratch(n_loc, rows, ff, slice_d, deep):
    bf16 = jnp.bfloat16
    return [
        pltpu.VMEM((deep, ff, slice_d), bf16), pltpu.SemaphoreType.DMA((deep,)),
        pltpu.VMEM((n_loc * rows, slice_d), bf16), pltpu.VMEM((n_loc * rows, slice_d), bf16),
    ]


def experts_up(place, near, blocks, w_held, w_up, w_down, topk):
    n_exp, n_seg = len(blocks), lax.axis_size("seg")
    n_loc, ff, width = w_down.shape
    tok = blocks[0].shape[0]
    tokens, slice_d = near[0].shape
    rows = up_to(SEND_CAP * n_exp, 16)
    tile_f = ff // 3
    wide = (n_seg - 2) * slice_d
    sizes = (n_exp, n_seg, n_loc, rows, tok, slice_d, tile_f, topk, len(w_held))
    bf16 = jnp.bfloat16
    vmem = lambda values: [(value, pltpu.VMEM) for value in values]
    outs = call(
        functools.partial(up_kernel, sizes),
        [(place, pltpu.SMEM)] + vmem(near) + vmem(blocks) + vmem(w_held)
        + [(w_up, pltpu.HBM), (w_down, pltpu.HBM)],
        [jax.ShapeDtypeStruct((tok, wide), bf16)] * n_exp
        + [jax.ShapeDtypeStruct((n_loc * rows, ff), bf16),
           jax.ShapeDtypeStruct((tokens, n_loc * rows), bf16),
           jax.ShapeDtypeStruct((n_loc * rows, 1), jnp.float32)]
        + [pltpu.VMEM(w.shape, bf16) for w in w_held],
        [pltpu.VMEM((n_loc * rows, tokens), bf16),
         pltpu.VMEM((tokens, wide), bf16),
         pltpu.VMEM((n_loc * rows, width), bf16),
         pltpu.VMEM((3, width, tile_f), bf16),
         pltpu.SemaphoreType.DMA((3,)),
         pltpu.SemaphoreType.DMA((len(w_held), n_loc)),
         pltpu.VMEM((n_loc * rows, slice_d), bf16), pltpu.VMEM((n_loc * rows, slice_d), bf16)],
        15, flops=2 * n_loc * 256 * width * ff, moved=n_loc * ff * width * 2,
        aliases=[(3 + n_exp + i, n_exp + 3 + i) for i in range(len(w_held))],
    )
    return outs[:n_exp], outs[n_exp:n_exp + 3], outs[n_exp + 3:]


def experts_down(held, weights, n_loc, slice_d, dtype):
    hidden, pick_t, row_w = held
    rows, ff = hidden.shape[0] // n_loc, hidden.shape[1]
    bf16 = jnp.bfloat16
    return call(
        functools.partial(down_kernel, rows, n_loc),
        [(x, pltpu.VMEM) for x in (hidden, pick_t, row_w, weights)],
        [jax.ShapeDtypeStruct((pick_t.shape[0], slice_d), dtype)],
        [pltpu.VMEM((n_loc * rows, slice_d), bf16), pltpu.VMEM((n_loc * rows, slice_d), bf16)],
        16, flops=2 * n_loc * 256 * slice_d * ff,
    )[0]


def experts_own(place, held, w_down, slice_d):
    hidden, pick_t, row_w = held
    n_loc, ff, _ = w_down.shape
    rows = hidden.shape[0] // n_loc
    return call(
        functools.partial(own_kernel, rows),
        [(place, pltpu.SMEM)] + [(x, pltpu.VMEM) for x in (hidden, pick_t, row_w)]
        + [(w_down, pltpu.HBM)],
        [jax.ShapeDtypeStruct((pick_t.shape[0], slice_d), jnp.float32)],
        down_scratch(n_loc, rows, ff, slice_d, n_loc),
        16, flops=2 * n_loc * 256 * slice_d * ff, moved=2 * n_loc * ff * slice_d,
    )[0]


def total_of(parts):
    total = parts[0].astype(jnp.float32)
    for part in parts[1:]:
        total = total + part.astype(jnp.float32)
    return total


def staged(tokens, expert_ids, route_weight, w_up, w_down):
    n_exp = lax.axis_size("expert")
    n_seg = lax.axis_size("seg")
    tok, slice_d = tokens.shape
    topk = expert_ids.shape[1]
    far = range(2, n_seg)
    peers = range(1, n_exp)
    place = jnp.stack([lax.axis_index("seg"), lax.axis_index("expert")]).astype(jnp.int32)

    a = [hop(tokens, "seg", k) for k in far]
    b = [tokens] + [hop(tokens, "expert", k) for k in peers]
    routes = jnp.concatenate([expert_ids.T.astype(jnp.float32), route_weight.T], axis=0)
    route, held_0 = call(
        functools.partial(route_kernel, topk),
        [(place, pltpu.SMEM), (routes, pltpu.VMEM), (w_up, pltpu.HBM)],
        [jax.ShapeDtypeStruct((tok, LANES), tokens.dtype), pltpu.VMEM(w_up.shape[1:], w_up.dtype)],
        [pltpu.SemaphoreType.DMA], 20,
    )
    near = join(b, 0)
    e = hop(near, "seg", 1)
    block = join(a + [route], 1)
    blocks = [block] + [hop(block, "expert", k) for k in peers]
    w_held = [held_0, *fetch(w_up, 1, n_seg - 1, block, place)]

    c, held, ahead = experts_up(place, [near, e], blocks, w_held, w_up, w_down, topk)
    c = [c[0]] + [hop(c[k], "expert", k) for k in peers]
    n_loc = w_up.shape[0]
    g = hop(experts_down(held, ahead[-1], n_loc, slice_d, jnp.bfloat16), "seg", 1)
    own = experts_own(place, held, w_down, slice_d)
    total = total_of(c).astype(jnp.bfloat16)
    sent = [total[:, (k - 2) * slice_d:(k - 1) * slice_d] for k in far]
    d = [hop(x, "seg", k) for x, k in zip(sent, far)]
    own = total_of([own, g])
    mine = own[:tok]
    own = own.astype(jnp.bfloat16)
    h = [hop(own[k * tok:(k + 1) * tok], "expert", k) for k in peers]
    return total_of([mine] + h + d).astype(jnp.bfloat16)


def plain(tokens, expert_ids, route_weight, w_up, w_down):
    n_exp = lax.axis_size("expert")
    exp_local, width = w_up.shape[:2]
    n_experts = n_exp * exp_local
    topk = expert_ids.shape[1]
    tok_rows, width_seg = tokens.shape
    flat = expert_ids.reshape(-1)
    onehot = (flat[:, None] == jnp.arange(n_experts, dtype=jnp.int32)[None, :]).astype(jnp.int32)
    before = jnp.cumsum(onehot, axis=0) - onehot
    target = flat * SEND_CAP + jnp.sum(before * onehot, axis=1)
    norm_weight = route_weight / jnp.sum(route_weight, axis=1, keepdims=True)
    buffer = jnp.zeros((n_experts * SEND_CAP, width_seg), tokens.dtype)
    packed = buffer.at[target].set(jnp.repeat(tokens, topk, axis=0))
    packed = packed.reshape(n_exp, exp_local * SEND_CAP, width_seg)
    arrived = lax.all_to_all(packed, "expert", split_axis=0, concat_axis=0, tiled=True)
    piece = lax.all_gather(arrived, "seg", axis=2, tiled=True)
    block = piece.reshape(n_exp, exp_local, SEND_CAP, width)
    up_sum = jnp.einsum("sekd,edf->eskf", block, w_up, preferred_element_type=jnp.float32)
    hidden = jax.nn.silu(up_sum).astype(jnp.bfloat16)
    partial_out = jnp.einsum("eskf,efd->sekd", hidden, w_down, preferred_element_type=jnp.float32)
    partial_out = partial_out.reshape(n_exp, exp_local * SEND_CAP, width)
    returned = lax.all_to_all(partial_out, "expert", split_axis=0, concat_axis=0, tiled=True)
    picked = returned.reshape(n_experts * SEND_CAP, width)[target]
    weighted = (picked * norm_weight.reshape(-1)[:, None]).reshape(tok_rows, topk, width).sum(axis=1)
    return lax.psum_scatter(weighted, "seg", scatter_dimension=1, tiled=True).astype(jnp.bfloat16)


def shards(tokens, expert_ids, route_weight, w_up, w_down):
    n_exp, n_seg = lax.axis_size("expert"), lax.axis_size("seg")
    n_loc, ff, width = w_down.shape
    slice_d = tokens.shape[1]
    paired = n_exp & (n_exp - 1) == 0 and n_seg & (n_seg - 1) == 0
    room = n_loc >= n_seg > 2 and n_loc * slice_d <= width and ff % (3 * LANES) == 0
    if not (paired and room and slice_d % LANES == 0 and ff % slice_d == 0):
        return plain(tokens, expert_ids, route_weight, w_up, w_down)
    return staged(tokens, expert_ids, route_weight, w_up, w_down)


def solution(mesh):
    placed = (
        P(("dp", "expert"), "seg"),
        P(("dp", "expert"), None),
        P(("dp", "expert"), None),
        P("expert", None, "seg"),
        P("expert", "seg", None),
    )
    return jax.shard_map(
        shards, mesh=mesh, in_specs=placed, out_specs=P(("dp", "expert"), "seg"), check_vma=False
    )
```

```python
import functools

import jax
import jax.numpy as jnp
from jax import lax
from jax.experimental import pallas as pl
from jax.experimental.pallas import tpu as pltpu
from jax.sharding import PartitionSpec as P


SEND_CAP = 21
LANES = 128


def hop(value, axis, k):
    n = lax.axis_size(axis)
    return lax.ppermute(value, axis, [(i, i ^ k) for i in range(n)])


def up_to(value, multiple):
    return -(-value // multiple) * multiple


def call(body, ins, outs, scratch, limit, flops=0, moved=0, aliases=()):
    return pl.pallas_call(
        body,
        in_specs=[pl.BlockSpec(memory_space=space) for _, space in ins],
        out_specs=[pl.BlockSpec(memory_space=pltpu.VMEM) for _ in outs],
        out_shape=outs,
        scratch_shapes=scratch,
        input_output_aliases=dict(aliases),
        compiler_params=pltpu.CompilerParams(vmem_limit_bytes=limit << 20),
        cost_estimate=pl.CostEstimate(flops=flops, bytes_accessed=moved, transcendentals=0),
    )(*[value for value, _ in ins])


def route_kernel(topk, place, ids_hbm, route_hbm, w_up, out, weights, ids, route, sem, sems):
    small = [
        pltpu.make_async_copy(ids_hbm, ids, sems.at[0]),
        pltpu.make_async_copy(route_hbm, route, sems.at[1]),
    ]
    for x in small:
        x.start()
    copy = pltpu.make_async_copy(w_up.at[0], weights, sem)
    copy.start()
    for x in small:
        x.wait()
    tok = ids.shape[1]
    rows = up_to(3 * topk, 16)
    weight = route[...]
    norm = weight / jnp.sum(weight, axis=0, keepdims=True)
    high = norm.astype(jnp.bfloat16).astype(jnp.float32)
    info = jnp.concatenate([ids[...].astype(jnp.float32), high, norm - high], axis=0)
    info = jnp.concatenate([info, jnp.zeros((rows - 3 * topk, tok), jnp.float32)], axis=0)
    info = jnp.concatenate([info, jnp.zeros((rows, out.shape[1] - tok), jnp.float32)], axis=1)
    out[...] = jnp.zeros(out.shape, out.dtype)
    out[:rows, :] = info.astype(jnp.bfloat16)
    copy.wait()


def join_kernel(axis, *refs):
    at = 0
    for x in refs[:-1]:
        size = x.shape[axis]
        if axis:
            refs[-1][:, at:at + size] = x[...]
        else:
            refs[-1][at:at + size, :] = x[...]
        at += size


def join(values, axis):
    shape = list(values[0].shape)
    shape[axis] = sum(x.shape[axis] for x in values)
    return call(
        functools.partial(join_kernel, axis), [(x, pltpu.VMEM) for x in values],
        [jax.ShapeDtypeStruct(tuple(shape), values[0].dtype)], [], 4,
    )[0]


def fetch_kernel(lo, w_ref, after, place, *refs):
    outs, sem = refs[:-1], refs[-1]
    copies = [
        pltpu.make_async_copy(w_ref.at[lo + i], out, sem.at[i]) for i, out in enumerate(outs)
    ]
    for copy in copies:
        copy.start()
    for copy in copies:
        copy.wait()


def fetch(w, lo, hi, after, place):
    return call(
        functools.partial(fetch_kernel, lo),
        [(w, pltpu.HBM), (after, pltpu.HBM), (place, pltpu.SMEM)], [pltpu.VMEM(w.shape[1:], w.dtype)] * (hi - lo),
        [pltpu.SemaphoreType.DMA((hi - lo,))], 20, moved=2 * w[0].size * (hi - lo),
    )


def route_rows(info, n_loc, rows, topk, first_expert, pick, pick_t, row_w):
    tokens = pick.shape[1]
    info = info.astype(jnp.float32)
    ids = info[:topk]
    weights = info[topk:2 * topk] + info[2 * topk:3 * topk]
    earlier = (
        lax.broadcasted_iota(jnp.int32, (tokens, tokens), 0)
        < lax.broadcasted_iota(jnp.int32, (tokens, tokens), 1)
    ).astype(jnp.float32).astype(jnp.bfloat16)
    slot_of_row = lax.broadcasted_iota(jnp.int32, (rows, tokens), 0).astype(jnp.float32)
    for e in range(n_loc):
        here = (ids == (first_expert + e).astype(jnp.float32)).astype(jnp.float32)
        mask = jnp.sum(here, axis=0, keepdims=True)
        gain = jnp.sum(here * weights, axis=0, keepdims=True)
        before = jnp.dot(
            jnp.broadcast_to(mask, (16, tokens)).astype(jnp.bfloat16), earlier,
            preferred_element_type=jnp.float32,
        )
        chosen = jnp.where((slot_of_row == before[:1]) & (mask > 0.5), 1.0, 0.0)
        pick[e * rows:(e + 1) * rows, :] = chosen.astype(jnp.bfloat16)
        row_w[e * rows:(e + 1) * rows, :] = jnp.sum(chosen * gain, axis=1, keepdims=True)
    pick_t[...] = jnp.transpose(pick[...].astype(jnp.float32)).astype(jnp.bfloat16)


def piece(e, ff, slice_d):
    per = ff // slice_d
    return slice(e // per * ff, (e // per + 1) * ff), slice(e % per * slice_d, (e % per + 1) * slice_d)


def slice_copies(place, j, slice_d, w_down, ahead, sem):
    n_loc, ff, _ = w_down.shape
    at = pl.multiple_of((place[0] ^ j) * slice_d, LANES)
    return [
        pltpu.make_async_copy(
            w_down.at[e, :, pl.ds(at, slice_d)], ahead.at[piece(e, ff, slice_d)], sem.at[e]
        )
        for e in range(n_loc)
    ]


def down_rows(hidden, weight, row_w, at, high, low):
    result = jnp.dot(hidden[at, :], weight, preferred_element_type=jnp.float32)
    result = result * row_w[at, :]
    upper = result.astype(jnp.bfloat16)
    high[at, :] = upper
    low[at, :] = (result - upper.astype(jnp.float32)).astype(jnp.bfloat16)


def combine(pick_t, high, low):
    total = jnp.dot(pick_t[...], high[...], preferred_element_type=jnp.float32)
    return total + jnp.dot(pick_t[...], low[...], preferred_element_type=jnp.float32)


def down_slice(weights, hidden, pick_t, row_w, rows, n_loc, slice_d, high, low):
    for e in range(n_loc):
        at = slice(e * rows, (e + 1) * rows)
        weight = weights[piece(e, hidden.shape[1], slice_d)]
        down_rows(hidden, weight, row_w, at, high, low)
    return combine(pick_t, high, low)


def up_kernel(sizes, place, *refs):
    n_exp, n_seg, n_loc, rows, tok, slice_d, tile_f, topk, n_held = sizes
    far = n_seg - 2
    near, refs = refs[:2], refs[2:]
    blocks, refs = refs[:n_exp], refs[n_exp:]
    w_held, refs = refs[:n_held], refs[n_held:]
    (w_up, w_down), refs = refs[:2], refs[2:]
    outs, refs = refs[:n_exp], refs[n_exp:]
    (hidden, pick_t, row_w), room, refs = refs[:3], refs[3:3 + n_held], refs[3 + n_held:]
    pick, joined, packed, buf_u, sem_u, sem_a, high, low = refs
    per = w_up.shape[2] // tile_f
    tiles = (n_loc - n_held) * per
    deep_u = buf_u.shape[0]

    def tile_u(t):
        cols = pl.ds(pl.multiple_of(lax.rem(t, per) * tile_f, LANES), tile_f)
        slot = lax.rem(t, deep_u)
        return pltpu.make_async_copy(
            w_up.at[n_held + lax.div(t, per), :, cols], buf_u.at[slot], sem_u.at[slot]
        )

    for t in range(min(deep_u, tiles)):
        tile_u(jnp.int32(t)).start()
    wide = far * slice_d
    for k in range(n_exp):
        joined[k * tok:(k + 1) * tok, :] = blocks[k][:, :wide]
    info = jnp.concatenate([x[:up_to(3 * topk, 16), wide:wide + tok] for x in blocks], axis=1)
    route_rows(info, n_loc, rows, topk, place[1] * n_loc, pick, pick_t, row_w)
    for j in range(n_seg):
        x = near[j][...] if j < 2 else joined[:, (j - 2) * slice_d:(j - 1) * slice_d]
        part = jnp.dot(pick[...], x, preferred_element_type=jnp.float32)
        at = pl.multiple_of((place[0] ^ j) * slice_d, LANES)
        packed[:, pl.ds(at, slice_d)] = part.astype(jnp.bfloat16)

    def up(at, cols, weight):
        value = jnp.dot(packed[at, :], weight, preferred_element_type=jnp.float32)
        value = value / (1.0 + jnp.exp(-value))
        hidden[at, cols] = value.astype(jnp.bfloat16)

    slices = list(range(2, n_seg)) + [1]
    copies = [
        slice_copies(place, j, slice_d, w_down, room[i], sem_a.at[i]) for i, j in enumerate(slices)
    ]
    for e, held in enumerate(w_held):
        half = held.shape[1] // 2

        def from_held(f, carry, e=e, held=held):
            cols = pl.ds(pl.multiple_of(f * half, LANES), half)
            up(slice(e * rows, (e + 1) * rows), cols, held[:, cols])
            return carry

        lax.fori_loop(0, 2, from_held, 0)
        for copy in copies[e]:
            copy.start()

    def from_ring(t, carry):
        tile_u(t).wait()
        at = pl.ds(pl.multiple_of((n_held + lax.div(t, per)) * rows, 16), rows)
        cols = pl.ds(pl.multiple_of(lax.rem(t, per) * tile_f, LANES), tile_f)
        up(at, cols, buf_u[lax.rem(t, deep_u)])

        @pl.when(t + deep_u < tiles)
        def _():
            tile_u(t + deep_u).start()

        return carry

    lax.fori_loop(0, tiles, from_ring, 0)
    for i in range(far):
        for copy in copies[i]:
            copy.wait()
        total = down_slice(room[i], hidden, pick_t, row_w, rows, n_loc, slice_d, high, low)
        total = total.astype(jnp.bfloat16)
        for k, out in enumerate(outs):
            out[:, i * slice_d:(i + 1) * slice_d] = total[k * tok:(k + 1) * tok]
    for copy in copies[far]:
        copy.wait()


def down_kernel(rows, n_loc, hidden, pick_t, row_w, weights, out, high, low):
    total = down_slice(weights, hidden, pick_t, row_w, rows, n_loc, out.shape[1], high, low)
    out[...] = total.astype(out.dtype)


def own_kernel(rows, place, hidden, pick_t, row_w, w_down, out, buf, sem, high, low):
    n_loc = w_down.shape[0]
    at = pl.multiple_of(place[0] * out.shape[1], LANES)
    copies = [
        pltpu.make_async_copy(w_down.at[e, :, pl.ds(at, out.shape[1])], buf.at[e], sem.at[e])
        for e in range(n_loc)
    ]
    for copy in copies:
        copy.start()
    for e, copy in enumerate(copies):
        copy.wait()
        down_rows(hidden, buf[e], row_w, slice(e * rows, (e + 1) * rows), high, low)
    out[...] = combine(pick_t, high, low).astype(out.dtype)


def down_scratch(n_loc, rows, ff, slice_d, deep):
    bf16 = jnp.bfloat16
    return [
        pltpu.VMEM((deep, ff, slice_d), bf16), pltpu.SemaphoreType.DMA((deep,)),
        pltpu.VMEM((n_loc * rows, slice_d), bf16), pltpu.VMEM((n_loc * rows, slice_d), bf16),
    ]


def experts_up(place, near, blocks, w_held, w_up, w_down, topk):
    n_exp, n_seg = len(blocks), lax.axis_size("seg")
    n_loc, ff, width = w_down.shape
    tok = blocks[0].shape[0]
    tokens, slice_d = near[0].shape
    rows = up_to(SEND_CAP * n_exp, 16)
    tile_f = ff // 3
    wide = (n_seg - 2) * slice_d
    sizes = (n_exp, n_seg, n_loc, rows, tok, slice_d, tile_f, topk, len(w_held))
    bf16 = jnp.bfloat16
    vmem = lambda values: [(value, pltpu.VMEM) for value in values]
    outs = call(
        functools.partial(up_kernel, sizes),
        [(place, pltpu.SMEM)] + vmem(near) + vmem(blocks) + vmem(w_held)
        + [(w_up, pltpu.HBM), (w_down, pltpu.HBM)],
        [jax.ShapeDtypeStruct((tok, wide), bf16)] * n_exp
        + [jax.ShapeDtypeStruct((n_loc * rows, ff), bf16),
           jax.ShapeDtypeStruct((tokens, n_loc * rows), bf16),
           jax.ShapeDtypeStruct((n_loc * rows, 1), jnp.float32)]
        + [pltpu.VMEM(w.shape, bf16) for w in w_held],
        [pltpu.VMEM((n_loc * rows, tokens), bf16),
         pltpu.VMEM((tokens, wide), bf16),
         pltpu.VMEM((n_loc * rows, width), bf16),
         pltpu.VMEM((3, width, tile_f), bf16),
         pltpu.SemaphoreType.DMA((3,)),
         pltpu.SemaphoreType.DMA((len(w_held), n_loc)),
         pltpu.VMEM((n_loc * rows, slice_d), bf16), pltpu.VMEM((n_loc * rows, slice_d), bf16)],
        15, flops=2 * n_loc * 256 * width * ff, moved=n_loc * ff * width * 2,
        aliases=[(3 + n_exp + i, n_exp + 3 + i) for i in range(len(w_held))],
    )
    return outs[:n_exp], outs[n_exp:n_exp + 3], outs[n_exp + 3:]


def experts_down(held, weights, n_loc, slice_d, dtype):
    hidden, pick_t, row_w = held
    rows, ff = hidden.shape[0] // n_loc, hidden.shape[1]
    bf16 = jnp.bfloat16
    return call(
        functools.partial(down_kernel, rows, n_loc),
        [(x, pltpu.VMEM) for x in (hidden, pick_t, row_w, weights)],
        [jax.ShapeDtypeStruct((pick_t.shape[0], slice_d), dtype)],
        [pltpu.VMEM((n_loc * rows, slice_d), bf16), pltpu.VMEM((n_loc * rows, slice_d), bf16)],
        16, flops=2 * n_loc * 256 * slice_d * ff,
    )[0]


def experts_own(place, held, w_down, slice_d):
    hidden, pick_t, row_w = held
    n_loc, ff, _ = w_down.shape
    rows = hidden.shape[0] // n_loc
    return call(
        functools.partial(own_kernel, rows),
        [(place, pltpu.SMEM)] + [(x, pltpu.VMEM) for x in (hidden, pick_t, row_w)]
        + [(w_down, pltpu.HBM)],
        [jax.ShapeDtypeStruct((pick_t.shape[0], slice_d), jnp.float32)],
        down_scratch(n_loc, rows, ff, slice_d, n_loc),
        16, flops=2 * n_loc * 256 * slice_d * ff, moved=2 * n_loc * ff * slice_d,
    )[0]


def total_of(parts):
    total = parts[0].astype(jnp.float32)
    for part in parts[1:]:
        total = total + part.astype(jnp.float32)
    return total


def staged(tokens, expert_ids, route_weight, w_up, w_down):
    n_exp = lax.axis_size("expert")
    n_seg = lax.axis_size("seg")
    tok, slice_d = tokens.shape
    topk = expert_ids.shape[1]
    far = range(2, n_seg)
    peers = range(1, n_exp)
    place = jnp.stack([lax.axis_index("seg"), lax.axis_index("expert")]).astype(jnp.int32)

    a = [hop(tokens, "seg", k) for k in far]
    b = [tokens] + [hop(tokens, "expert", k) for k in peers]
    ids = pltpu.with_memory_space_constraint(expert_ids.T, pltpu.HBM)
    weights = pltpu.with_memory_space_constraint(route_weight.T, pltpu.HBM)
    route, held_0 = call(
        functools.partial(route_kernel, topk),
        [(place, pltpu.SMEM), (ids, pltpu.HBM), (weights, pltpu.HBM), (w_up, pltpu.HBM)],
        [jax.ShapeDtypeStruct((tok, LANES), tokens.dtype), pltpu.VMEM(w_up.shape[1:], w_up.dtype)],
        [pltpu.VMEM((topk, tok), jnp.int32), pltpu.VMEM((topk, tok), jnp.float32),
         pltpu.SemaphoreType.DMA, pltpu.SemaphoreType.DMA((2,))], 20,
    )
    near = join(b, 0)
    e = hop(near, "seg", 1)
    block = join(a + [route], 1)
    blocks = [block] + [hop(block, "expert", k) for k in peers]
    w_held = [held_0, *fetch(w_up, 1, n_seg - 1, block, place)]

    c, held, ahead = experts_up(place, [near, e], blocks, w_held, w_up, w_down, topk)
    c = [c[0]] + [hop(c[k], "expert", k) for k in peers]
    n_loc = w_up.shape[0]
    g = hop(experts_down(held, ahead[-1], n_loc, slice_d, jnp.bfloat16), "seg", 1)
    own = experts_own(place, held, w_down, slice_d)
    total = total_of(c).astype(jnp.bfloat16)
    sent = [total[:, (k - 2) * slice_d:(k - 1) * slice_d] for k in far]
    d = [hop(x, "seg", k) for x, k in zip(sent, far)]
    own = total_of([own, g])
    mine = own[:tok]
    own = own.astype(jnp.bfloat16)
    h = [hop(own[k * tok:(k + 1) * tok], "expert", k) for k in peers]
    return total_of([mine] + h + d).astype(jnp.bfloat16)


def plain(tokens, expert_ids, route_weight, w_up, w_down):
    n_exp = lax.axis_size("expert")
    exp_local, width = w_up.shape[:2]
    n_experts = n_exp * exp_local
    topk = expert_ids.shape[1]
    tok_rows, width_seg = tokens.shape
    flat = expert_ids.reshape(-1)
    onehot = (flat[:, None] == jnp.arange(n_experts, dtype=jnp.int32)[None, :]).astype(jnp.int32)
    before = jnp.cumsum(onehot, axis=0) - onehot
    target = flat * SEND_CAP + jnp.sum(before * onehot, axis=1)
    norm_weight = route_weight / jnp.sum(route_weight, axis=1, keepdims=True)
    buffer = jnp.zeros((n_experts * SEND_CAP, width_seg), tokens.dtype)
    packed = buffer.at[target].set(jnp.repeat(tokens, topk, axis=0))
    packed = packed.reshape(n_exp, exp_local * SEND_CAP, width_seg)
    arrived = lax.all_to_all(packed, "expert", split_axis=0, concat_axis=0, tiled=True)
    piece = lax.all_gather(arrived, "seg", axis=2, tiled=True)
    block = piece.reshape(n_exp, exp_local, SEND_CAP, width)
    up_sum = jnp.einsum("sekd,edf->eskf", block, w_up, preferred_element_type=jnp.float32)
    hidden = jax.nn.silu(up_sum).astype(jnp.bfloat16)
    partial_out = jnp.einsum("eskf,efd->sekd", hidden, w_down, preferred_element_type=jnp.float32)
    partial_out = partial_out.reshape(n_exp, exp_local * SEND_CAP, width)
    returned = lax.all_to_all(partial_out, "expert", split_axis=0, concat_axis=0, tiled=True)
    picked = returned.reshape(n_experts * SEND_CAP, width)[target]
    weighted = (picked * norm_weight.reshape(-1)[:, None]).reshape(tok_rows, topk, width).sum(axis=1)
    return lax.psum_scatter(weighted, "seg", scatter_dimension=1, tiled=True).astype(jnp.bfloat16)


def shards(tokens, expert_ids, route_weight, w_up, w_down):
    n_exp, n_seg = lax.axis_size("expert"), lax.axis_size("seg")
    n_loc, ff, width = w_down.shape
    slice_d = tokens.shape[1]
    paired = n_exp & (n_exp - 1) == 0 and n_seg & (n_seg - 1) == 0
    room = n_loc >= n_seg > 2 and n_loc * slice_d <= width and ff % (3 * LANES) == 0
    if not (paired and room and slice_d % LANES == 0 and ff % slice_d == 0):
        return plain(tokens, expert_ids, route_weight, w_up, w_down)
    return staged(tokens, expert_ids, route_weight, w_up, w_down)


def solution(mesh):
    placed = (
        P(("dp", "expert"), "seg"),
        P(("dp", "expert"), None),
        P(("dp", "expert"), None),
        P("expert", None, "seg"),
        P("expert", "seg", None),
    )
    return jax.shard_map(
        shards, mesh=mesh, in_specs=placed, out_specs=P(("dp", "expert"), "seg"), check_vma=False
    )
```

```python
import functools

import jax
import jax.numpy as jnp
from jax import lax
from jax.experimental import pallas as pl
from jax.experimental.pallas import tpu as pltpu
from jax.sharding import PartitionSpec as P


SEND_CAP = 21
LANES = 128


def hop(value, axis, k):
    n = lax.axis_size(axis)
    return lax.ppermute(value, axis, [(i, i ^ k) for i in range(n)])


def up_to(value, multiple):
    return -(-value // multiple) * multiple


def call(body, ins, outs, scratch, limit, flops=0, moved=0, aliases=()):
    return pl.pallas_call(
        body,
        in_specs=[pl.BlockSpec(memory_space=space) for _, space in ins],
        out_specs=[pl.BlockSpec(memory_space=pltpu.VMEM) for _ in outs],
        out_shape=outs,
        scratch_shapes=scratch,
        input_output_aliases=dict(aliases),
        compiler_params=pltpu.CompilerParams(vmem_limit_bytes=limit << 20),
        cost_estimate=pl.CostEstimate(flops=flops, bytes_accessed=moved, transcendentals=0),
    )(*[value for value, _ in ins])


def route_kernel(topk, place, ids_hbm, route_hbm, w_up, out, weights, ids, route, sem, sems):
    small = [
        pltpu.make_async_copy(ids_hbm, ids, sems.at[0]),
        pltpu.make_async_copy(route_hbm, route, sems.at[1]),
    ]
    for x in small:
        x.start()
    copy = pltpu.make_async_copy(w_up.at[0], weights, sem)
    copy.start()
    for x in small:
        x.wait()
    tok = ids.shape[1]
    rows = up_to(3 * topk, 16)
    weight = route[...]
    norm = weight / jnp.sum(weight, axis=0, keepdims=True)
    high = norm.astype(jnp.bfloat16).astype(jnp.float32)
    info = jnp.concatenate([ids[...].astype(jnp.float32), high, norm - high], axis=0)
    info = jnp.concatenate([info, jnp.zeros((rows - 3 * topk, tok), jnp.float32)], axis=0)
    info = jnp.concatenate([info, jnp.zeros((rows, out.shape[1] - tok), jnp.float32)], axis=1)
    out[...] = jnp.zeros(out.shape, out.dtype)
    out[:rows, :] = info.astype(jnp.bfloat16)
    copy.wait()


def join_kernel(axis, *refs):
    at = 0
    for x in refs[:-1]:
        size = x.shape[axis]
        if axis:
            refs[-1][:, at:at + size] = x[...]
        else:
            refs[-1][at:at + size, :] = x[...]
        at += size


def join(values, axis):
    shape = list(values[0].shape)
    shape[axis] = sum(x.shape[axis] for x in values)
    return call(
        functools.partial(join_kernel, axis), [(x, pltpu.VMEM) for x in values],
        [jax.ShapeDtypeStruct(tuple(shape), values[0].dtype)], [], 4,
    )[0]


def fetch_kernel(lo, w_ref, after, place, *refs):
    outs, sem = refs[:-1], refs[-1]
    copies = [
        pltpu.make_async_copy(w_ref.at[lo + i], out, sem.at[i]) for i, out in enumerate(outs)
    ]
    for copy in copies:
        copy.start()
    for copy in copies:
        copy.wait()


def fetch(w, lo, hi, after, place):
    return call(
        functools.partial(fetch_kernel, lo),
        [(w, pltpu.HBM), (after, pltpu.HBM), (place, pltpu.SMEM)], [pltpu.VMEM(w.shape[1:], w.dtype)] * (hi - lo),
        [pltpu.SemaphoreType.DMA((hi - lo,))], 20, moved=2 * w[0].size * (hi - lo),
    )


def route_rows(info, n_loc, rows, topk, first_expert, pick, pick_t, row_w):
    tokens = pick.shape[1]
    info = info.astype(jnp.float32)
    ids = info[:topk]
    weights = info[topk:2 * topk] + info[2 * topk:3 * topk]
    earlier = (
        lax.broadcasted_iota(jnp.int32, (tokens, tokens), 0)
        < lax.broadcasted_iota(jnp.int32, (tokens, tokens), 1)
    ).astype(jnp.float32).astype(jnp.bfloat16)
    slot_of_row = lax.broadcasted_iota(jnp.int32, (rows, tokens), 0).astype(jnp.float32)
    for e in range(n_loc):
        here = (ids == (first_expert + e).astype(jnp.float32)).astype(jnp.float32)
        mask = jnp.sum(here, axis=0, keepdims=True)
        gain = jnp.sum(here * weights, axis=0, keepdims=True)
        before = jnp.dot(
            jnp.broadcast_to(mask, (16, tokens)).astype(jnp.bfloat16), earlier,
            preferred_element_type=jnp.float32,
        )
        chosen = jnp.where((slot_of_row == before[:1]) & (mask > 0.5), 1.0, 0.0)
        pick[e * rows:(e + 1) * rows, :] = chosen.astype(jnp.bfloat16)
        row_w[e * rows:(e + 1) * rows, :] = jnp.sum(chosen * gain, axis=1, keepdims=True)
    pick_t[...] = jnp.transpose(pick[...].astype(jnp.float32)).astype(jnp.bfloat16)


def piece(e, ff, slice_d):
    per = ff // slice_d
    return slice(e // per * ff, (e // per + 1) * ff), slice(e % per * slice_d, (e % per + 1) * slice_d)


def slice_copies(place, j, slice_d, w_down, ahead, sem):
    n_loc, ff, _ = w_down.shape
    at = pl.multiple_of((place[0] ^ j) * slice_d, LANES)
    return [
        pltpu.make_async_copy(
            w_down.at[e, :, pl.ds(at, slice_d)], ahead.at[piece(e, ff, slice_d)], sem.at[e]
        )
        for e in range(n_loc)
    ]


def down_rows(hidden, weight, row_w, at, high, low):
    result = jnp.dot(hidden[at, :], weight, preferred_element_type=jnp.float32)
    result = result * row_w[at, :]
    upper = result.astype(jnp.bfloat16)
    high[at, :] = upper
    low[at, :] = (result - upper.astype(jnp.float32)).astype(jnp.bfloat16)


def combine(pick_t, high, low):
    total = jnp.dot(pick_t[...], high[...], preferred_element_type=jnp.float32)
    return total + jnp.dot(pick_t[...], low[...], preferred_element_type=jnp.float32)


def down_slice(weights, hidden, pick_t, row_w, rows, n_loc, slice_d, high, low):
    for e in range(n_loc):
        at = slice(e * rows, (e + 1) * rows)
        weight = weights[piece(e, hidden.shape[1], slice_d)]
        down_rows(hidden, weight, row_w, at, high, low)
    return combine(pick_t, high, low)


def up_kernel(sizes, place, *refs):
    n_exp, n_seg, n_loc, rows, tok, slice_d, tile_f, topk, n_held = sizes
    far = n_seg - 2
    near, refs = refs[:2], refs[2:]
    blocks, refs = refs[:n_exp], refs[n_exp:]
    w_held, refs = refs[:n_held], refs[n_held:]
    (w_up, w_down), refs = refs[:2], refs[2:]
    outs, refs = refs[:n_exp], refs[n_exp:]
    (hidden, pick_t, row_w), room, refs = refs[:3], refs[3:3 + n_held], refs[3 + n_held:]
    pick, joined, packed, buf_u, sem_u, sem_a, high, low = refs
    per = w_up.shape[2] // tile_f
    tiles = (n_loc - n_held) * per
    deep_u = buf_u.shape[0]

    def tile_u(t):
        cols = pl.ds(pl.multiple_of(lax.rem(t, per) * tile_f, LANES), tile_f)
        slot = lax.rem(t, deep_u)
        return pltpu.make_async_copy(
            w_up.at[n_held + lax.div(t, per), :, cols], buf_u.at[slot], sem_u.at[slot]
        )

    for t in range(min(deep_u, tiles)):
        tile_u(jnp.int32(t)).start()
    wide = far * slice_d
    for k in range(n_exp):
        joined[k * tok:(k + 1) * tok, :] = blocks[k][:, :wide]
    info = jnp.concatenate([x[:up_to(3 * topk, 16), wide:wide + tok] for x in blocks], axis=1)
    route_rows(info, n_loc, rows, topk, place[1] * n_loc, pick, pick_t, row_w)
    for j in range(n_seg):
        x = near[j][...] if j < 2 else joined[:, (j - 2) * slice_d:(j - 1) * slice_d]
        part = jnp.dot(pick[...], x, preferred_element_type=jnp.float32)
        at = pl.multiple_of((place[0] ^ j) * slice_d, LANES)
        packed[:, pl.ds(at, slice_d)] = part.astype(jnp.bfloat16)

    def up(at, cols, weight):
        value = jnp.dot(packed[at, :], weight, preferred_element_type=jnp.float32)
        value = value / (1.0 + jnp.exp(-value))
        hidden[at, cols] = value.astype(jnp.bfloat16)

    slices = list(range(2, n_seg)) + [1]
    copies = [
        slice_copies(place, j, slice_d, w_down, room[i], sem_a.at[i]) for i, j in enumerate(slices)
    ]
    for e, held in enumerate(w_held):
        half = held.shape[1] // 2

        @pl.when(place[0] >= 0)
        def _(e=e, held=held, half=half):
            for f in range(2):
                cols = slice(f * half, (f + 1) * half)
                up(slice(e * rows, (e + 1) * rows), cols, held[:, cols])

        for copy in copies[e]:
            copy.start()

    def from_ring(t, carry):
        tile_u(t).wait()
        at = pl.ds(pl.multiple_of((n_held + lax.div(t, per)) * rows, 16), rows)
        cols = pl.ds(pl.multiple_of(lax.rem(t, per) * tile_f, LANES), tile_f)
        up(at, cols, buf_u[lax.rem(t, deep_u)])

        @pl.when(t + deep_u < tiles)
        def _():
            tile_u(t + deep_u).start()

        return carry

    lax.fori_loop(0, tiles, from_ring, 0)
    for i in range(far):
        for copy in copies[i]:
            copy.wait()
        total = down_slice(room[i], hidden, pick_t, row_w, rows, n_loc, slice_d, high, low)
        total = total.astype(jnp.bfloat16)
        for k, out in enumerate(outs):
            out[:, i * slice_d:(i + 1) * slice_d] = total[k * tok:(k + 1) * tok]
    for copy in copies[far]:
        copy.wait()


def down_kernel(rows, n_loc, hidden, pick_t, row_w, weights, out, high, low):
    total = down_slice(weights, hidden, pick_t, row_w, rows, n_loc, out.shape[1], high, low)
    out[...] = total.astype(out.dtype)


def own_kernel(rows, place, hidden, pick_t, row_w, w_down, out, buf, sem, high, low):
    n_loc = w_down.shape[0]
    at = pl.multiple_of(place[0] * out.shape[1], LANES)
    copies = [
        pltpu.make_async_copy(w_down.at[e, :, pl.ds(at, out.shape[1])], buf.at[e], sem.at[e])
        for e in range(n_loc)
    ]
    for copy in copies:
        copy.start()
    for e, copy in enumerate(copies):
        copy.wait()
        down_rows(hidden, buf[e], row_w, slice(e * rows, (e + 1) * rows), high, low)
    out[...] = combine(pick_t, high, low).astype(out.dtype)


def down_scratch(n_loc, rows, ff, slice_d, deep):
    bf16 = jnp.bfloat16
    return [
        pltpu.VMEM((deep, ff, slice_d), bf16), pltpu.SemaphoreType.DMA((deep,)),
        pltpu.VMEM((n_loc * rows, slice_d), bf16), pltpu.VMEM((n_loc * rows, slice_d), bf16),
    ]


def experts_up(place, near, blocks, w_held, w_up, w_down, topk):
    n_exp, n_seg = len(blocks), lax.axis_size("seg")
    n_loc, ff, width = w_down.shape
    tok = blocks[0].shape[0]
    tokens, slice_d = near[0].shape
    rows = up_to(SEND_CAP * n_exp, 16)
    tile_f = ff // 3
    wide = (n_seg - 2) * slice_d
    sizes = (n_exp, n_seg, n_loc, rows, tok, slice_d, tile_f, topk, len(w_held))
    bf16 = jnp.bfloat16
    vmem = lambda values: [(value, pltpu.VMEM) for value in values]
    outs = call(
        functools.partial(up_kernel, sizes),
        [(place, pltpu.SMEM)] + vmem(near) + vmem(blocks) + vmem(w_held)
        + [(w_up, pltpu.HBM), (w_down, pltpu.HBM)],
        [jax.ShapeDtypeStruct((tok, wide), bf16)] * n_exp
        + [jax.ShapeDtypeStruct((n_loc * rows, ff), bf16),
           jax.ShapeDtypeStruct((tokens, n_loc * rows), bf16),
           jax.ShapeDtypeStruct((n_loc * rows, 1), jnp.float32)]
        + [pltpu.VMEM(w.shape, bf16) for w in w_held],
        [pltpu.VMEM((n_loc * rows, tokens), bf16),
         pltpu.VMEM((tokens, wide), bf16),
         pltpu.VMEM((n_loc * rows, width), bf16),
         pltpu.VMEM((3, width, tile_f), bf16),
         pltpu.SemaphoreType.DMA((3,)),
         pltpu.SemaphoreType.DMA((len(w_held), n_loc)),
         pltpu.VMEM((n_loc * rows, slice_d), bf16), pltpu.VMEM((n_loc * rows, slice_d), bf16)],
        15, flops=2 * n_loc * 256 * width * ff, moved=n_loc * ff * width * 2,
        aliases=[(3 + n_exp + i, n_exp + 3 + i) for i in range(len(w_held))],
    )
    return outs[:n_exp], outs[n_exp:n_exp + 3], outs[n_exp + 3:]


def experts_down(held, weights, n_loc, slice_d, dtype):
    hidden, pick_t, row_w = held
    rows, ff = hidden.shape[0] // n_loc, hidden.shape[1]
    bf16 = jnp.bfloat16
    return call(
        functools.partial(down_kernel, rows, n_loc),
        [(x, pltpu.VMEM) for x in (hidden, pick_t, row_w, weights)],
        [jax.ShapeDtypeStruct((pick_t.shape[0], slice_d), dtype)],
        [pltpu.VMEM((n_loc * rows, slice_d), bf16), pltpu.VMEM((n_loc * rows, slice_d), bf16)],
        16, flops=2 * n_loc * 256 * slice_d * ff,
    )[0]


def experts_own(place, held, w_down, slice_d):
    hidden, pick_t, row_w = held
    n_loc, ff, _ = w_down.shape
    rows = hidden.shape[0] // n_loc
    return call(
        functools.partial(own_kernel, rows),
        [(place, pltpu.SMEM)] + [(x, pltpu.VMEM) for x in (hidden, pick_t, row_w)]
        + [(w_down, pltpu.HBM)],
        [jax.ShapeDtypeStruct((pick_t.shape[0], slice_d), jnp.float32)],
        down_scratch(n_loc, rows, ff, slice_d, n_loc),
        16, flops=2 * n_loc * 256 * slice_d * ff, moved=2 * n_loc * ff * slice_d,
    )[0]


def total_of(parts):
    total = parts[0].astype(jnp.float32)
    for part in parts[1:]:
        total = total + part.astype(jnp.float32)
    return total


def staged(tokens, expert_ids, route_weight, w_up, w_down):
    n_exp = lax.axis_size("expert")
    n_seg = lax.axis_size("seg")
    tok, slice_d = tokens.shape
    topk = expert_ids.shape[1]
    far = range(2, n_seg)
    peers = range(1, n_exp)
    place = jnp.stack([lax.axis_index("seg"), lax.axis_index("expert")]).astype(jnp.int32)

    a = [hop(tokens, "seg", k) for k in far]
    b = [tokens] + [hop(tokens, "expert", k) for k in peers]
    ids = pltpu.with_memory_space_constraint(expert_ids.T, pltpu.HBM)
    weights = pltpu.with_memory_space_constraint(route_weight.T, pltpu.HBM)
    route, held_0 = call(
        functools.partial(route_kernel, topk),
        [(place, pltpu.SMEM), (ids, pltpu.HBM), (weights, pltpu.HBM), (w_up, pltpu.HBM)],
        [jax.ShapeDtypeStruct((tok, LANES), tokens.dtype), pltpu.VMEM(w_up.shape[1:], w_up.dtype)],
        [pltpu.VMEM((topk, tok), jnp.int32), pltpu.VMEM((topk, tok), jnp.float32),
         pltpu.SemaphoreType.DMA, pltpu.SemaphoreType.DMA((2,))], 20,
    )
    near = join(b, 0)
    e = hop(near, "seg", 1)
    block = join(a + [route], 1)
    blocks = [block] + [hop(block, "expert", k) for k in peers]
    w_held = [held_0, *fetch(w_up, 1, n_seg - 1, block, place)]

    c, held, ahead = experts_up(place, [near, e], blocks, w_held, w_up, w_down, topk)
    c = [c[0]] + [hop(c[k], "expert", k) for k in peers]
    n_loc = w_up.shape[0]
    g = hop(experts_down(held, ahead[-1], n_loc, slice_d, jnp.bfloat16), "seg", 1)
    own = experts_own(place, held, w_down, slice_d)
    total = total_of(c).astype(jnp.bfloat16)
    sent = [total[:, (k - 2) * slice_d:(k - 1) * slice_d] for k in far]
    d = [hop(x, "seg", k) for x, k in zip(sent, far)]
    own = total_of([own, g])
    mine = own[:tok]
    own = own.astype(jnp.bfloat16)
    h = [hop(own[k * tok:(k + 1) * tok], "expert", k) for k in peers]
    return total_of([mine] + h + d).astype(jnp.bfloat16)


def plain(tokens, expert_ids, route_weight, w_up, w_down):
    n_exp = lax.axis_size("expert")
    exp_local, width = w_up.shape[:2]
    n_experts = n_exp * exp_local
    topk = expert_ids.shape[1]
    tok_rows, width_seg = tokens.shape
    flat = expert_ids.reshape(-1)
    onehot = (flat[:, None] == jnp.arange(n_experts, dtype=jnp.int32)[None, :]).astype(jnp.int32)
    before = jnp.cumsum(onehot, axis=0) - onehot
    target = flat * SEND_CAP + jnp.sum(before * onehot, axis=1)
    norm_weight = route_weight / jnp.sum(route_weight, axis=1, keepdims=True)
    buffer = jnp.zeros((n_experts * SEND_CAP, width_seg), tokens.dtype)
    packed = buffer.at[target].set(jnp.repeat(tokens, topk, axis=0))
    packed = packed.reshape(n_exp, exp_local * SEND_CAP, width_seg)
    arrived = lax.all_to_all(packed, "expert", split_axis=0, concat_axis=0, tiled=True)
    piece = lax.all_gather(arrived, "seg", axis=2, tiled=True)
    block = piece.reshape(n_exp, exp_local, SEND_CAP, width)
    up_sum = jnp.einsum("sekd,edf->eskf", block, w_up, preferred_element_type=jnp.float32)
    hidden = jax.nn.silu(up_sum).astype(jnp.bfloat16)
    partial_out = jnp.einsum("eskf,efd->sekd", hidden, w_down, preferred_element_type=jnp.float32)
    partial_out = partial_out.reshape(n_exp, exp_local * SEND_CAP, width)
    returned = lax.all_to_all(partial_out, "expert", split_axis=0, concat_axis=0, tiled=True)
    picked = returned.reshape(n_experts * SEND_CAP, width)[target]
    weighted = (picked * norm_weight.reshape(-1)[:, None]).reshape(tok_rows, topk, width).sum(axis=1)
    return lax.psum_scatter(weighted, "seg", scatter_dimension=1, tiled=True).astype(jnp.bfloat16)


def shards(tokens, expert_ids, route_weight, w_up, w_down):
    n_exp, n_seg = lax.axis_size("expert"), lax.axis_size("seg")
    n_loc, ff, width = w_down.shape
    slice_d = tokens.shape[1]
    paired = n_exp & (n_exp - 1) == 0 and n_seg & (n_seg - 1) == 0
    room = n_loc >= n_seg > 2 and n_loc * slice_d <= width and ff % (3 * LANES) == 0
    if not (paired and room and slice_d % LANES == 0 and ff % slice_d == 0):
        return plain(tokens, expert_ids, route_weight, w_up, w_down)
    return staged(tokens, expert_ids, route_weight, w_up, w_down)


def solution(mesh):
    placed = (
        P(("dp", "expert"), "seg"),
        P(("dp", "expert"), None),
        P(("dp", "expert"), None),
        P("expert", None, "seg"),
        P("expert", "seg", None),
    )
    return jax.shard_map(
        shards, mesh=mesh, in_specs=placed, out_specs=P(("dp", "expert"), "seg"), check_vma=False
    )
```

```python
import functools

import jax
import jax.numpy as jnp
from jax import lax
from jax.experimental import pallas as pl
from jax.experimental.pallas import tpu as pltpu
from jax.sharding import PartitionSpec as P


SEND_CAP = 21
LANES = 128


def hop(value, axis, k):
    n = lax.axis_size(axis)
    return lax.ppermute(value, axis, [(i, i ^ k) for i in range(n)])


def up_to(value, multiple):
    return -(-value // multiple) * multiple


def call(body, ins, outs, scratch, limit, flops=0, moved=0, aliases=()):
    return pl.pallas_call(
        body,
        in_specs=[pl.BlockSpec(memory_space=space) for _, space in ins],
        out_specs=[pl.BlockSpec(memory_space=pltpu.VMEM) for _ in outs],
        out_shape=outs,
        scratch_shapes=scratch,
        input_output_aliases=dict(aliases),
        compiler_params=pltpu.CompilerParams(vmem_limit_bytes=limit << 20),
        cost_estimate=pl.CostEstimate(flops=flops, bytes_accessed=moved, transcendentals=0),
    )(*[value for value, _ in ins])


def route_kernel(topk, place, ids_hbm, route_hbm, w_up, out, weights, ids, route, sem, sems):
    small = [
        pltpu.make_async_copy(ids_hbm, ids, sems.at[0]),
        pltpu.make_async_copy(route_hbm, route, sems.at[1]),
    ]
    for x in small:
        x.start()
    copy = pltpu.make_async_copy(w_up.at[0], weights, sem)
    copy.start()
    for x in small:
        x.wait()
    tok = ids.shape[1]
    rows = up_to(3 * topk, 16)
    weight = route[...]
    norm = weight / jnp.sum(weight, axis=0, keepdims=True)
    high = norm.astype(jnp.bfloat16).astype(jnp.float32)
    info = jnp.concatenate([ids[...].astype(jnp.float32), high, norm - high], axis=0)
    info = jnp.concatenate([info, jnp.zeros((rows - 3 * topk, tok), jnp.float32)], axis=0)
    info = jnp.concatenate([info, jnp.zeros((rows, out.shape[1] - tok), jnp.float32)], axis=1)
    out[...] = jnp.zeros(out.shape, out.dtype)
    out[:rows, :] = info.astype(jnp.bfloat16)
    copy.wait()


def join_kernel(axis, *refs):
    at = 0
    for x in refs[:-1]:
        size = x.shape[axis]
        if axis:
            refs[-1][:, at:at + size] = x[...]
        else:
            refs[-1][at:at + size, :] = x[...]
        at += size


def join(values, axis):
    shape = list(values[0].shape)
    shape[axis] = sum(x.shape[axis] for x in values)
    return call(
        functools.partial(join_kernel, axis), [(x, pltpu.VMEM) for x in values],
        [jax.ShapeDtypeStruct(tuple(shape), values[0].dtype)], [], 4,
    )[0]


def fetch_kernel(lo, w_ref, after, place, *refs):
    outs, sem = refs[:-1], refs[-1]
    copies = [
        pltpu.make_async_copy(w_ref.at[lo + i], out, sem.at[i]) for i, out in enumerate(outs)
    ]
    for copy in copies:
        copy.start()
    for copy in copies:
        copy.wait()


def fetch(w, lo, hi, after, place):
    return call(
        functools.partial(fetch_kernel, lo),
        [(w, pltpu.HBM), (after, pltpu.HBM), (place, pltpu.SMEM)], [pltpu.VMEM(w.shape[1:], w.dtype)] * (hi - lo),
        [pltpu.SemaphoreType.DMA((hi - lo,))], 20, moved=2 * w[0].size * (hi - lo),
    )


def route_rows(info, n_loc, rows, topk, first_expert, pick, pick_t, row_w):
    tokens = pick.shape[1]
    info = info.astype(jnp.float32)
    ids = info[:topk]
    weights = info[topk:2 * topk] + info[2 * topk:3 * topk]
    earlier = (
        lax.broadcasted_iota(jnp.int32, (tokens, tokens), 0)
        < lax.broadcasted_iota(jnp.int32, (tokens, tokens), 1)
    ).astype(jnp.float32).astype(jnp.bfloat16)
    slot_of_row = lax.broadcasted_iota(jnp.int32, (rows, tokens), 0).astype(jnp.float32)
    for e in range(n_loc):
        here = (ids == (first_expert + e).astype(jnp.float32)).astype(jnp.float32)
        mask = jnp.sum(here, axis=0, keepdims=True)
        gain = jnp.sum(here * weights, axis=0, keepdims=True)
        before = jnp.dot(
            jnp.broadcast_to(mask, (16, tokens)).astype(jnp.bfloat16), earlier,
            preferred_element_type=jnp.float32,
        )
        chosen = jnp.where((slot_of_row == before[:1]) & (mask > 0.5), 1.0, 0.0)
        pick[e * rows:(e + 1) * rows, :] = chosen.astype(jnp.bfloat16)
        row_w[e * rows:(e + 1) * rows, :] = jnp.sum(chosen * gain, axis=1, keepdims=True)
    pick_t[...] = jnp.transpose(pick[...].astype(jnp.float32)).astype(jnp.bfloat16)


def piece(e, ff, slice_d):
    per = ff // slice_d
    return slice(e // per * ff, (e // per + 1) * ff), slice(e % per * slice_d, (e % per + 1) * slice_d)


def slice_copies(place, j, slice_d, w_down, ahead, sem):
    n_loc, ff, _ = w_down.shape
    at = pl.multiple_of((place[0] ^ j) * slice_d, LANES)
    return [
        pltpu.make_async_copy(
            w_down.at[e, :, pl.ds(at, slice_d)], ahead.at[piece(e, ff, slice_d)], sem.at[e]
        )
        for e in range(n_loc)
    ]


def down_rows(hidden, weight, row_w, at, high):
    result = jnp.dot(hidden[at, :], weight, preferred_element_type=jnp.float32)
    high[at, :] = (result * row_w[at, :]).astype(jnp.bfloat16)


def combine(pick_t, high):
    return jnp.dot(pick_t[...], high[...], preferred_element_type=jnp.float32)


def down_slice(weights, hidden, pick_t, row_w, rows, n_loc, slice_d, high):
    for e in range(n_loc):
        at = slice(e * rows, (e + 1) * rows)
        weight = weights[piece(e, hidden.shape[1], slice_d)]
        down_rows(hidden, weight, row_w, at, high)
    return combine(pick_t, high)


def up_kernel(sizes, place, *refs):
    n_exp, n_seg, n_loc, rows, tok, slice_d, tile_f, topk, n_held = sizes
    far = n_seg - 2
    near, refs = refs[:2], refs[2:]
    blocks, refs = refs[:n_exp], refs[n_exp:]
    w_held, refs = refs[:n_held], refs[n_held:]
    (w_up, w_down), refs = refs[:2], refs[2:]
    outs, refs = refs[:n_exp], refs[n_exp:]
    (hidden, pick_t, row_w), room, refs = refs[:3], refs[3:3 + n_held], refs[3 + n_held:]
    pick, joined, packed, buf_u, sem_u, sem_a, high = refs
    per = w_up.shape[2] // tile_f
    tiles = (n_loc - n_held) * per
    deep_u = buf_u.shape[0]

    def tile_u(t):
        cols = pl.ds(pl.multiple_of(lax.rem(t, per) * tile_f, LANES), tile_f)
        slot = lax.rem(t, deep_u)
        return pltpu.make_async_copy(
            w_up.at[n_held + lax.div(t, per), :, cols], buf_u.at[slot], sem_u.at[slot]
        )

    for t in range(min(deep_u, tiles)):
        tile_u(jnp.int32(t)).start()
    wide = far * slice_d
    for k in range(n_exp):
        joined[k * tok:(k + 1) * tok, :] = blocks[k][:, :wide]
    info = jnp.concatenate([x[:up_to(3 * topk, 16), wide:wide + tok] for x in blocks], axis=1)
    route_rows(info, n_loc, rows, topk, place[1] * n_loc, pick, pick_t, row_w)
    for j in range(n_seg):
        x = near[j][...] if j < 2 else joined[:, (j - 2) * slice_d:(j - 1) * slice_d]
        part = jnp.dot(pick[...], x, preferred_element_type=jnp.float32)
        at = pl.multiple_of((place[0] ^ j) * slice_d, LANES)
        packed[:, pl.ds(at, slice_d)] = part.astype(jnp.bfloat16)

    def up(at, cols, weight):
        value = jnp.dot(packed[at, :], weight, preferred_element_type=jnp.float32)
        value = value / (1.0 + jnp.exp(-value))
        hidden[at, cols] = value.astype(jnp.bfloat16)

    slices = list(range(2, n_seg)) + [1]
    copies = [
        slice_copies(place, j, slice_d, w_down, room[i], sem_a.at[i]) for i, j in enumerate(slices)
    ]
    for e, held in enumerate(w_held):
        half = held.shape[1] // 2

        @pl.when(place[0] >= 0)
        def _(e=e, held=held, half=half):
            for f in range(2):
                cols = slice(f * half, (f + 1) * half)
                up(slice(e * rows, (e + 1) * rows), cols, held[:, cols])

        for copy in copies[e]:
            copy.start()

    def from_ring(t, carry):
        tile_u(t).wait()
        at = pl.ds(pl.multiple_of((n_held + lax.div(t, per)) * rows, 16), rows)
        cols = pl.ds(pl.multiple_of(lax.rem(t, per) * tile_f, LANES), tile_f)
        up(at, cols, buf_u[lax.rem(t, deep_u)])

        @pl.when(t + deep_u < tiles)
        def _():
            tile_u(t + deep_u).start()

        return carry

    lax.fori_loop(0, tiles, from_ring, 0)
    for i in range(far):
        for copy in copies[i]:
            copy.wait()
        total = down_slice(room[i], hidden, pick_t, row_w, rows, n_loc, slice_d, high)
        total = total.astype(jnp.bfloat16)
        for k, out in enumerate(outs):
            out[:, i * slice_d:(i + 1) * slice_d] = total[k * tok:(k + 1) * tok]
    for copy in copies[far]:
        copy.wait()


def down_kernel(rows, n_loc, hidden, pick_t, row_w, weights, out, high):
    total = down_slice(weights, hidden, pick_t, row_w, rows, n_loc, out.shape[1], high)
    out[...] = total.astype(out.dtype)


def own_kernel(rows, place, hidden, pick_t, row_w, w_down, out, buf, sem, high):
    n_loc = w_down.shape[0]
    at = pl.multiple_of(place[0] * out.shape[1], LANES)
    copies = [
        pltpu.make_async_copy(w_down.at[e, :, pl.ds(at, out.shape[1])], buf.at[e], sem.at[e])
        for e in range(n_loc)
    ]
    for copy in copies:
        copy.start()
    for e, copy in enumerate(copies):
        copy.wait()
        down_rows(hidden, buf[e], row_w, slice(e * rows, (e + 1) * rows), high)
    out[...] = combine(pick_t, high).astype(out.dtype)


def down_scratch(n_loc, rows, ff, slice_d, deep):
    bf16 = jnp.bfloat16
    return [
        pltpu.VMEM((deep, ff, slice_d), bf16), pltpu.SemaphoreType.DMA((deep,)),
        pltpu.VMEM((n_loc * rows, slice_d), bf16),
    ]


def experts_up(place, near, blocks, w_held, w_up, w_down, topk):
    n_exp, n_seg = len(blocks), lax.axis_size("seg")
    n_loc, ff, width = w_down.shape
    tok = blocks[0].shape[0]
    tokens, slice_d = near[0].shape
    rows = up_to(SEND_CAP * n_exp, 16)
    tile_f = ff // 3
    wide = (n_seg - 2) * slice_d
    sizes = (n_exp, n_seg, n_loc, rows, tok, slice_d, tile_f, topk, len(w_held))
    bf16 = jnp.bfloat16
    vmem = lambda values: [(value, pltpu.VMEM) for value in values]
    outs = call(
        functools.partial(up_kernel, sizes),
        [(place, pltpu.SMEM)] + vmem(near) + vmem(blocks) + vmem(w_held)
        + [(w_up, pltpu.HBM), (w_down, pltpu.HBM)],
        [jax.ShapeDtypeStruct((tok, wide), bf16)] * n_exp
        + [jax.ShapeDtypeStruct((n_loc * rows, ff), bf16),
           jax.ShapeDtypeStruct((tokens, n_loc * rows), bf16),
           jax.ShapeDtypeStruct((n_loc * rows, 1), jnp.float32)]
        + [pltpu.VMEM(w.shape, bf16) for w in w_held],
        [pltpu.VMEM((n_loc * rows, tokens), bf16),
         pltpu.VMEM((tokens, wide), bf16),
         pltpu.VMEM((n_loc * rows, width), bf16),
         pltpu.VMEM((3, width, tile_f), bf16),
         pltpu.SemaphoreType.DMA((3,)),
         pltpu.SemaphoreType.DMA((len(w_held), n_loc)),
         pltpu.VMEM((n_loc * rows, slice_d), bf16)],
        15, flops=2 * n_loc * 256 * width * ff, moved=n_loc * ff * width * 2,
        aliases=[(3 + n_exp + i, n_exp + 3 + i) for i in range(len(w_held))],
    )
    return outs[:n_exp], outs[n_exp:n_exp + 3], outs[n_exp + 3:]


def experts_down(held, weights, n_loc, slice_d, dtype):
    hidden, pick_t, row_w = held
    rows, ff = hidden.shape[0] // n_loc, hidden.shape[1]
    bf16 = jnp.bfloat16
    return call(
        functools.partial(down_kernel, rows, n_loc),
        [(x, pltpu.VMEM) for x in (hidden, pick_t, row_w, weights)],
        [jax.ShapeDtypeStruct((pick_t.shape[0], slice_d), dtype)],
        [pltpu.VMEM((n_loc * rows, slice_d), bf16)],
        16, flops=2 * n_loc * 256 * slice_d * ff,
    )[0]


def experts_own(place, held, w_down, slice_d):
    hidden, pick_t, row_w = held
    n_loc, ff, _ = w_down.shape
    rows = hidden.shape[0] // n_loc
    return call(
        functools.partial(own_kernel, rows),
        [(place, pltpu.SMEM)] + [(x, pltpu.VMEM) for x in (hidden, pick_t, row_w)]
        + [(w_down, pltpu.HBM)],
        [jax.ShapeDtypeStruct((pick_t.shape[0], slice_d), jnp.float32)],
        down_scratch(n_loc, rows, ff, slice_d, n_loc),
        16, flops=2 * n_loc * 256 * slice_d * ff, moved=2 * n_loc * ff * slice_d,
    )[0]


def total_of(parts):
    total = parts[0].astype(jnp.float32)
    for part in parts[1:]:
        total = total + part.astype(jnp.float32)
    return total


def staged(tokens, expert_ids, route_weight, w_up, w_down):
    n_exp = lax.axis_size("expert")
    n_seg = lax.axis_size("seg")
    tok, slice_d = tokens.shape
    topk = expert_ids.shape[1]
    far = range(2, n_seg)
    peers = range(1, n_exp)
    place = jnp.stack([lax.axis_index("seg"), lax.axis_index("expert")]).astype(jnp.int32)

    a = [hop(tokens, "seg", k) for k in far]
    b = [tokens] + [hop(tokens, "expert", k) for k in peers]
    ids = pltpu.with_memory_space_constraint(expert_ids.T, pltpu.HBM)
    weights = pltpu.with_memory_space_constraint(route_weight.T, pltpu.HBM)
    route, held_0 = call(
        functools.partial(route_kernel, topk),
        [(place, pltpu.SMEM), (ids, pltpu.HBM), (weights, pltpu.HBM), (w_up, pltpu.HBM)],
        [jax.ShapeDtypeStruct((tok, LANES), tokens.dtype), pltpu.VMEM(w_up.shape[1:], w_up.dtype)],
        [pltpu.VMEM((topk, tok), jnp.int32), pltpu.VMEM((topk, tok), jnp.float32),
         pltpu.SemaphoreType.DMA, pltpu.SemaphoreType.DMA((2,))], 20,
    )
    near = join(b, 0)
    e = hop(near, "seg", 1)
    block = join(a + [route], 1)
    blocks = [block] + [hop(block, "expert", k) for k in peers]
    w_held = [held_0, *fetch(w_up, 1, n_seg - 1, block, place)]

    c, held, ahead = experts_up(place, [near, e], blocks, w_held, w_up, w_down, topk)
    c = [c[0]] + [hop(c[k], "expert", k) for k in peers]
    n_loc = w_up.shape[0]
    g = hop(experts_down(held, ahead[-1], n_loc, slice_d, jnp.bfloat16), "seg", 1)
    own = experts_own(place, held, w_down, slice_d)
    total = total_of(c).astype(jnp.bfloat16)
    sent = [total[:, (k - 2) * slice_d:(k - 1) * slice_d] for k in far]
    d = [hop(x, "seg", k) for x, k in zip(sent, far)]
    own = total_of([own, g])
    mine = own[:tok]
    own = own.astype(jnp.bfloat16)
    h = [hop(own[k * tok:(k + 1) * tok], "expert", k) for k in peers]
    return total_of([mine] + h + d).astype(jnp.bfloat16)


def plain(tokens, expert_ids, route_weight, w_up, w_down):
    n_exp = lax.axis_size("expert")
    exp_local, width = w_up.shape[:2]
    n_experts = n_exp * exp_local
    topk = expert_ids.shape[1]
    tok_rows, width_seg = tokens.shape
    flat = expert_ids.reshape(-1)
    onehot = (flat[:, None] == jnp.arange(n_experts, dtype=jnp.int32)[None, :]).astype(jnp.int32)
    before = jnp.cumsum(onehot, axis=0) - onehot
    target = flat * SEND_CAP + jnp.sum(before * onehot, axis=1)
    norm_weight = route_weight / jnp.sum(route_weight, axis=1, keepdims=True)
    buffer = jnp.zeros((n_experts * SEND_CAP, width_seg), tokens.dtype)
    packed = buffer.at[target].set(jnp.repeat(tokens, topk, axis=0))
    packed = packed.reshape(n_exp, exp_local * SEND_CAP, width_seg)
    arrived = lax.all_to_all(packed, "expert", split_axis=0, concat_axis=0, tiled=True)
    piece = lax.all_gather(arrived, "seg", axis=2, tiled=True)
    block = piece.reshape(n_exp, exp_local, SEND_CAP, width)
    up_sum = jnp.einsum("sekd,edf->eskf", block, w_up, preferred_element_type=jnp.float32)
    hidden = jax.nn.silu(up_sum).astype(jnp.bfloat16)
    partial_out = jnp.einsum("eskf,efd->sekd", hidden, w_down, preferred_element_type=jnp.float32)
    partial_out = partial_out.reshape(n_exp, exp_local * SEND_CAP, width)
    returned = lax.all_to_all(partial_out, "expert", split_axis=0, concat_axis=0, tiled=True)
    picked = returned.reshape(n_experts * SEND_CAP, width)[target]
    weighted = (picked * norm_weight.reshape(-1)[:, None]).reshape(tok_rows, topk, width).sum(axis=1)
    return lax.psum_scatter(weighted, "seg", scatter_dimension=1, tiled=True).astype(jnp.bfloat16)


def shards(tokens, expert_ids, route_weight, w_up, w_down):
    n_exp, n_seg = lax.axis_size("expert"), lax.axis_size("seg")
    n_loc, ff, width = w_down.shape
    slice_d = tokens.shape[1]
    paired = n_exp & (n_exp - 1) == 0 and n_seg & (n_seg - 1) == 0
    room = n_loc >= n_seg > 2 and n_loc * slice_d <= width and ff % (3 * LANES) == 0
    if not (paired and room and slice_d % LANES == 0 and ff % slice_d == 0):
        return plain(tokens, expert_ids, route_weight, w_up, w_down)
    return staged(tokens, expert_ids, route_weight, w_up, w_down)


def solution(mesh):
    placed = (
        P(("dp", "expert"), "seg"),
        P(("dp", "expert"), None),
        P(("dp", "expert"), None),
        P("expert", None, "seg"),
        P("expert", "seg", None),
    )
    return jax.shard_map(
        shards, mesh=mesh, in_specs=placed, out_specs=P(("dp", "expert"), "seg"), check_vma=False
    )
```

```python
import functools

import jax
import jax.numpy as jnp
from jax import lax
from jax.experimental import pallas as pl
from jax.experimental.pallas import tpu as pltpu
from jax.sharding import PartitionSpec as P


SEND_CAP = 21
LANES = 128


def hop(value, axis, k):
    n = lax.axis_size(axis)
    return lax.ppermute(value, axis, [(i, i ^ k) for i in range(n)])


def up_to(value, multiple):
    return -(-value // multiple) * multiple


def call(body, ins, outs, scratch, limit, flops=0, moved=0, aliases=()):
    return pl.pallas_call(
        body,
        in_specs=[pl.BlockSpec(memory_space=space) for _, space in ins],
        out_specs=[pl.BlockSpec(memory_space=pltpu.VMEM) for _ in outs],
        out_shape=outs,
        scratch_shapes=scratch,
        input_output_aliases=dict(aliases),
        compiler_params=pltpu.CompilerParams(vmem_limit_bytes=limit << 20),
        cost_estimate=pl.CostEstimate(flops=flops, bytes_accessed=moved, transcendentals=0),
    )(*[value for value, _ in ins])


def route_kernel(topk, place, ids_hbm, route_hbm, w_up, out, weights, ids, route, sem, sems):
    small = [
        pltpu.make_async_copy(ids_hbm, ids, sems.at[0]),
        pltpu.make_async_copy(route_hbm, route, sems.at[1]),
    ]
    for x in small:
        x.start()
    copy = pltpu.make_async_copy(w_up.at[0], weights, sem)
    copy.start()
    for x in small:
        x.wait()
    tok = ids.shape[1]
    rows = up_to(3 * topk, 16)
    weight = route[...]
    norm = weight / jnp.sum(weight, axis=0, keepdims=True)
    high = norm.astype(jnp.bfloat16).astype(jnp.float32)
    info = jnp.concatenate([ids[...].astype(jnp.float32), high, norm - high], axis=0)
    info = jnp.concatenate([info, jnp.zeros((rows - 3 * topk, tok), jnp.float32)], axis=0)
    info = jnp.concatenate([info, jnp.zeros((rows, out.shape[1] - tok), jnp.float32)], axis=1)
    out[...] = jnp.zeros(out.shape, out.dtype)
    out[:rows, :] = info.astype(jnp.bfloat16)
    copy.wait()


def join_kernel(axis, *refs):
    at = 0
    for x in refs[:-1]:
        size = x.shape[axis]
        if axis:
            refs[-1][:, at:at + size] = x[...]
        else:
            refs[-1][at:at + size, :] = x[...]
        at += size


def join(values, axis):
    shape = list(values[0].shape)
    shape[axis] = sum(x.shape[axis] for x in values)
    return call(
        functools.partial(join_kernel, axis), [(x, pltpu.VMEM) for x in values],
        [jax.ShapeDtypeStruct(tuple(shape), values[0].dtype)], [], 4,
    )[0]


def fetch_kernel(lo, w_ref, after, place, *refs):
    outs, sem = refs[:-1], refs[-1]
    copies = [
        pltpu.make_async_copy(w_ref.at[lo + i], out, sem.at[i]) for i, out in enumerate(outs)
    ]
    for copy in copies:
        copy.start()
    for copy in copies:
        copy.wait()


def fetch(w, lo, hi, after, place):
    return call(
        functools.partial(fetch_kernel, lo),
        [(w, pltpu.HBM), (after, pltpu.HBM), (place, pltpu.SMEM)], [pltpu.VMEM(w.shape[1:], w.dtype)] * (hi - lo),
        [pltpu.SemaphoreType.DMA((hi - lo,))], 20, moved=2 * w[0].size * (hi - lo),
    )


def route_rows(info, n_loc, rows, topk, first_expert, pick, pick_t, row_w):
    tokens = pick.shape[1]
    info = info.astype(jnp.float32)
    ids = info[:topk]
    weights = info[topk:2 * topk] + info[2 * topk:3 * topk]
    earlier = (
        lax.broadcasted_iota(jnp.int32, (tokens, tokens), 0)
        < lax.broadcasted_iota(jnp.int32, (tokens, tokens), 1)
    ).astype(jnp.float32).astype(jnp.bfloat16)
    slot_of_row = lax.broadcasted_iota(jnp.int32, (rows, tokens), 0).astype(jnp.float32)
    for e in range(n_loc):
        here = (ids == (first_expert + e).astype(jnp.float32)).astype(jnp.float32)
        mask = jnp.sum(here, axis=0, keepdims=True)
        gain = jnp.sum(here * weights, axis=0, keepdims=True)
        before = jnp.dot(
            jnp.broadcast_to(mask, (16, tokens)).astype(jnp.bfloat16), earlier,
            preferred_element_type=jnp.float32,
        )
        chosen = jnp.where((slot_of_row == before[:1]) & (mask > 0.5), 1.0, 0.0)
        pick[e * rows:(e + 1) * rows, :] = chosen.astype(jnp.bfloat16)
        row_w[e * rows:(e + 1) * rows, :] = jnp.sum(chosen * gain, axis=1, keepdims=True)
    pick_t[...] = jnp.transpose(pick[...].astype(jnp.float32)).astype(jnp.bfloat16)


def piece(e, ff, slice_d):
    per = ff // slice_d
    return slice(e // per * ff, (e // per + 1) * ff), slice(e % per * slice_d, (e % per + 1) * slice_d)


def slice_copies(place, j, slice_d, w_down, ahead, sem):
    n_loc, ff, _ = w_down.shape
    at = pl.multiple_of((place[0] ^ j) * slice_d, LANES)
    return [
        pltpu.make_async_copy(
            w_down.at[e, :, pl.ds(at, slice_d)], ahead.at[piece(e, ff, slice_d)], sem.at[e]
        )
        for e in range(n_loc)
    ]


def down_rows(hidden, weight, row_w, at, high):
    result = jnp.dot(hidden[at, :], weight, preferred_element_type=jnp.float32)
    high[at, :] = (result * row_w[at, :]).astype(jnp.bfloat16)


def combine(pick_t, high):
    return jnp.dot(pick_t[...], high[...], preferred_element_type=jnp.float32)


def down_slice(weights, hidden, pick_t, row_w, rows, n_loc, slice_d, high):
    for e in range(n_loc):
        at = slice(e * rows, (e + 1) * rows)
        weight = weights[piece(e, hidden.shape[1], slice_d)]
        down_rows(hidden, weight, row_w, at, high)
    return combine(pick_t, high)


def up_kernel(sizes, place, *refs):
    n_exp, n_seg, n_loc, rows, tok, slice_d, tile_f, topk, n_held = sizes
    far = n_seg - 2
    near, refs = refs[:2], refs[2:]
    blocks, refs = refs[:n_exp], refs[n_exp:]
    w_held, refs = refs[:n_held], refs[n_held:]
    (w_up, w_down), refs = refs[:2], refs[2:]
    outs, refs = refs[:n_exp], refs[n_exp:]
    (hidden, pick_t, row_w), room, refs = refs[:3], refs[3:3 + n_held], refs[3 + n_held:]
    pick, joined, packed, buf_u, sem_u, sem_a, high = refs
    per = w_up.shape[2] // tile_f
    tiles = (n_loc - n_held) * per
    deep_u = buf_u.shape[0]

    def tile_u(t):
        cols = pl.ds(pl.multiple_of(lax.rem(t, per) * tile_f, LANES), tile_f)
        slot = lax.rem(t, deep_u)
        return pltpu.make_async_copy(
            w_up.at[n_held + lax.div(t, per), :, cols], buf_u.at[slot], sem_u.at[slot]
        )

    for t in range(min(deep_u, tiles)):
        tile_u(jnp.int32(t)).start()
    wide = far * slice_d
    for k in range(n_exp):
        joined[k * tok:(k + 1) * tok, :] = blocks[k][:, :wide]
    info = jnp.concatenate([x[:up_to(3 * topk, 16), wide:wide + tok] for x in blocks], axis=1)
    route_rows(info, n_loc, rows, topk, place[1] * n_loc, pick, pick_t, row_w)
    for j in range(n_seg):
        x = near[j][...] if j < 2 else joined[:, (j - 2) * slice_d:(j - 1) * slice_d]
        part = jnp.dot(pick[...], x, preferred_element_type=jnp.float32)
        at = pl.multiple_of((place[0] ^ j) * slice_d, LANES)
        packed[:, pl.ds(at, slice_d)] = part.astype(jnp.bfloat16)

    def up(at, cols, weight):
        value = jnp.dot(packed[at, :], weight, preferred_element_type=jnp.float32)
        value = value / (1.0 + jnp.exp(-value))
        hidden[at, cols] = value.astype(jnp.bfloat16)

    slices = list(range(2, n_seg)) + [1]
    copies = [
        slice_copies(place, j, slice_d, w_down, room[i], sem_a.at[i]) for i, j in enumerate(slices)
    ]
    for e, held in enumerate(w_held):
        half = held.shape[1] // 2

        @pl.when(place[0] >= 0)
        def _(e=e, held=held, half=half):
            for f in range(2):
                cols = slice(f * half, (f + 1) * half)
                up(slice(e * rows, (e + 1) * rows), cols, held[:, cols])

        for copy in copies[e]:
            copy.start()

    def from_ring(t, carry):
        tile_u(t).wait()
        at = pl.ds(pl.multiple_of((n_held + lax.div(t, per)) * rows, 16), rows)
        cols = pl.ds(pl.multiple_of(lax.rem(t, per) * tile_f, LANES), tile_f)
        up(at, cols, buf_u[lax.rem(t, deep_u)])

        @pl.when(t + deep_u < tiles)
        def _():
            tile_u(t + deep_u).start()

        return carry

    lax.fori_loop(0, tiles, from_ring, 0)
    for i in range(far):
        for copy in copies[i]:
            copy.wait()
        total = down_slice(room[i], hidden, pick_t, row_w, rows, n_loc, slice_d, high)
        total = total.astype(jnp.bfloat16)
        for k, out in enumerate(outs):
            out[:, i * slice_d:(i + 1) * slice_d] = total[k * tok:(k + 1) * tok]
    for copy in copies[far]:
        copy.wait()


def down_kernel(rows, n_loc, hidden, pick_t, row_w, weights, out, high):
    total = down_slice(weights, hidden, pick_t, row_w, rows, n_loc, out.shape[1], high)
    out[...] = total.astype(out.dtype)


def own_kernel(rows, place, hidden, pick_t, row_w, w_down, out, buf, sem, high):
    n_loc = w_down.shape[0]
    at = pl.multiple_of(place[0] * out.shape[1], LANES)
    copies = [
        pltpu.make_async_copy(w_down.at[e, :, pl.ds(at, out.shape[1])], buf.at[e], sem.at[e])
        for e in range(n_loc)
    ]
    for copy in copies:
        copy.start()
    half = n_loc // 2 * rows
    for e, copy in enumerate(copies):
        copy.wait()
        down_rows(hidden, buf[e], row_w, slice(e * rows, (e + 1) * rows), high)
        if e + 1 == n_loc // 2:
            out[...] = combine(pick_t.at[:, :half], high.at[:half])
    out[...] += combine(pick_t.at[:, half:], high.at[half:])


def down_scratch(n_loc, rows, ff, slice_d, deep):
    bf16 = jnp.bfloat16
    return [
        pltpu.VMEM((deep, ff, slice_d), bf16), pltpu.SemaphoreType.DMA((deep,)),
        pltpu.VMEM((n_loc * rows, slice_d), bf16),
    ]


def experts_up(place, near, blocks, w_held, w_up, w_down, topk):
    n_exp, n_seg = len(blocks), lax.axis_size("seg")
    n_loc, ff, width = w_down.shape
    tok = blocks[0].shape[0]
    tokens, slice_d = near[0].shape
    rows = up_to(SEND_CAP * n_exp, 16)
    tile_f = ff // 3
    wide = (n_seg - 2) * slice_d
    sizes = (n_exp, n_seg, n_loc, rows, tok, slice_d, tile_f, topk, len(w_held))
    bf16 = jnp.bfloat16
    vmem = lambda values: [(value, pltpu.VMEM) for value in values]
    outs = call(
        functools.partial(up_kernel, sizes),
        [(place, pltpu.SMEM)] + vmem(near) + vmem(blocks) + vmem(w_held)
        + [(w_up, pltpu.HBM), (w_down, pltpu.HBM)],
        [jax.ShapeDtypeStruct((tok, wide), bf16)] * n_exp
        + [jax.ShapeDtypeStruct((n_loc * rows, ff), bf16),
           jax.ShapeDtypeStruct((tokens, n_loc * rows), bf16),
           jax.ShapeDtypeStruct((n_loc * rows, 1), jnp.float32)]
        + [pltpu.VMEM(w.shape, bf16) for w in w_held],
        [pltpu.VMEM((n_loc * rows, tokens), bf16),
         pltpu.VMEM((tokens, wide), bf16),
         pltpu.VMEM((n_loc * rows, width), bf16),
         pltpu.VMEM((3, width, tile_f), bf16),
         pltpu.SemaphoreType.DMA((3,)),
         pltpu.SemaphoreType.DMA((len(w_held), n_loc)),
         pltpu.VMEM((n_loc * rows, slice_d), bf16)],
        15, flops=2 * n_loc * 256 * width * ff, moved=n_loc * ff * width * 2,
        aliases=[(3 + n_exp + i, n_exp + 3 + i) for i in range(len(w_held))],
    )
    return outs[:n_exp], outs[n_exp:n_exp + 3], outs[n_exp + 3:]


def experts_down(held, weights, n_loc, slice_d, dtype):
    hidden, pick_t, row_w = held
    rows, ff = hidden.shape[0] // n_loc, hidden.shape[1]
    bf16 = jnp.bfloat16
    return call(
        functools.partial(down_kernel, rows, n_loc),
        [(x, pltpu.VMEM) for x in (hidden, pick_t, row_w, weights)],
        [jax.ShapeDtypeStruct((pick_t.shape[0], slice_d), dtype)],
        [pltpu.VMEM((n_loc * rows, slice_d), bf16)],
        16, flops=2 * n_loc * 256 * slice_d * ff,
    )[0]


def experts_own(place, held, w_down, slice_d):
    hidden, pick_t, row_w = held
    n_loc, ff, _ = w_down.shape
    rows = hidden.shape[0] // n_loc
    return call(
        functools.partial(own_kernel, rows),
        [(place, pltpu.SMEM)] + [(x, pltpu.VMEM) for x in (hidden, pick_t, row_w)]
        + [(w_down, pltpu.HBM)],
        [jax.ShapeDtypeStruct((pick_t.shape[0], slice_d), jnp.float32)],
        down_scratch(n_loc, rows, ff, slice_d, n_loc),
        16, flops=2 * n_loc * 256 * slice_d * ff, moved=2 * n_loc * ff * slice_d,
    )[0]


def total_of(parts):
    total = parts[0].astype(jnp.float32)
    for part in parts[1:]:
        total = total + part.astype(jnp.float32)
    return total


def staged(tokens, expert_ids, route_weight, w_up, w_down):
    n_exp = lax.axis_size("expert")
    n_seg = lax.axis_size("seg")
    tok, slice_d = tokens.shape
    topk = expert_ids.shape[1]
    far = range(2, n_seg)
    peers = range(1, n_exp)
    place = jnp.stack([lax.axis_index("seg"), lax.axis_index("expert")]).astype(jnp.int32)

    a = [hop(tokens, "seg", k) for k in far]
    b = [tokens] + [hop(tokens, "expert", k) for k in peers]
    ids = pltpu.with_memory_space_constraint(expert_ids.T, pltpu.HBM)
    weights = pltpu.with_memory_space_constraint(route_weight.T, pltpu.HBM)
    route, held_0 = call(
        functools.partial(route_kernel, topk),
        [(place, pltpu.SMEM), (ids, pltpu.HBM), (weights, pltpu.HBM), (w_up, pltpu.HBM)],
        [jax.ShapeDtypeStruct((tok, LANES), tokens.dtype), pltpu.VMEM(w_up.shape[1:], w_up.dtype)],
        [pltpu.VMEM((topk, tok), jnp.int32), pltpu.VMEM((topk, tok), jnp.float32),
         pltpu.SemaphoreType.DMA, pltpu.SemaphoreType.DMA((2,))], 20,
    )
    near = join(b, 0)
    e = hop(near, "seg", 1)
    block = join(a + [route], 1)
    blocks = [block] + [hop(block, "expert", k) for k in peers]
    w_held = [held_0, *fetch(w_up, 1, n_seg - 1, block, place)]

    c, held, ahead = experts_up(place, [near, e], blocks, w_held, w_up, w_down, topk)
    c = [c[0]] + [hop(c[k], "expert", k) for k in peers]
    n_loc = w_up.shape[0]
    g = hop(experts_down(held, ahead[-1], n_loc, slice_d, jnp.bfloat16), "seg", 1)
    own = experts_own(place, held, w_down, slice_d)
    total = total_of(c).astype(jnp.bfloat16)
    sent = [total[:, (k - 2) * slice_d:(k - 1) * slice_d] for k in far]
    d = [hop(x, "seg", k) for x, k in zip(sent, far)]
    own = total_of([own, g])
    mine = own[:tok]
    own = own.astype(jnp.bfloat16)
    h = [hop(own[k * tok:(k + 1) * tok], "expert", k) for k in peers]
    return total_of([mine] + h + d).astype(jnp.bfloat16)


def plain(tokens, expert_ids, route_weight, w_up, w_down):
    n_exp = lax.axis_size("expert")
    exp_local, width = w_up.shape[:2]
    n_experts = n_exp * exp_local
    topk = expert_ids.shape[1]
    tok_rows, width_seg = tokens.shape
    flat = expert_ids.reshape(-1)
    onehot = (flat[:, None] == jnp.arange(n_experts, dtype=jnp.int32)[None, :]).astype(jnp.int32)
    before = jnp.cumsum(onehot, axis=0) - onehot
    target = flat * SEND_CAP + jnp.sum(before * onehot, axis=1)
    norm_weight = route_weight / jnp.sum(route_weight, axis=1, keepdims=True)
    buffer = jnp.zeros((n_experts * SEND_CAP, width_seg), tokens.dtype)
    packed = buffer.at[target].set(jnp.repeat(tokens, topk, axis=0))
    packed = packed.reshape(n_exp, exp_local * SEND_CAP, width_seg)
    arrived = lax.all_to_all(packed, "expert", split_axis=0, concat_axis=0, tiled=True)
    piece = lax.all_gather(arrived, "seg", axis=2, tiled=True)
    block = piece.reshape(n_exp, exp_local, SEND_CAP, width)
    up_sum = jnp.einsum("sekd,edf->eskf", block, w_up, preferred_element_type=jnp.float32)
    hidden = jax.nn.silu(up_sum).astype(jnp.bfloat16)
    partial_out = jnp.einsum("eskf,efd->sekd", hidden, w_down, preferred_element_type=jnp.float32)
    partial_out = partial_out.reshape(n_exp, exp_local * SEND_CAP, width)
    returned = lax.all_to_all(partial_out, "expert", split_axis=0, concat_axis=0, tiled=True)
    picked = returned.reshape(n_experts * SEND_CAP, width)[target]
    weighted = (picked * norm_weight.reshape(-1)[:, None]).reshape(tok_rows, topk, width).sum(axis=1)
    return lax.psum_scatter(weighted, "seg", scatter_dimension=1, tiled=True).astype(jnp.bfloat16)


def shards(tokens, expert_ids, route_weight, w_up, w_down):
    n_exp, n_seg = lax.axis_size("expert"), lax.axis_size("seg")
    n_loc, ff, width = w_down.shape
    slice_d = tokens.shape[1]
    paired = n_exp & (n_exp - 1) == 0 and n_seg & (n_seg - 1) == 0
    room = n_loc >= n_seg > 2 and n_loc * slice_d <= width and ff % (3 * LANES) == 0
    if not (paired and room and slice_d % LANES == 0 and ff % slice_d == 0):
        return plain(tokens, expert_ids, route_weight, w_up, w_down)
    return staged(tokens, expert_ids, route_weight, w_up, w_down)


def solution(mesh):
    placed = (
        P(("dp", "expert"), "seg"),
        P(("dp", "expert"), None),
        P(("dp", "expert"), None),
        P("expert", None, "seg"),
        P("expert", "seg", None),
    )
    return jax.shard_map(
        shards, mesh=mesh, in_specs=placed, out_specs=P(("dp", "expert"), "seg"), check_vma=False
    )
```
